32 devices in a mesh: dom: 32 (over z, y, x, core), rep: 1.
Axes of the slice: x: 2, y: 2, z: 4, core: 2. Of those that a mesh axis runs over, the one named last changes fastest.
Arguments:
- query_fde: bfloat16 [256, 10240], P(('rep', 'dom')), may hold values from -6 to 6
- doc_fde: bfloat16 [16384, 10240], P('dom'), may hold values from -0.0625 to 0.0625
- frontier_owner: int32 [3, 256, 16], P(None, ('rep', 'dom')), may hold values from 0 to 31, all different within a row; in each aligned block of 8 rows (0 to 7, 8 to 15, ..., all dimensions but the last counted through in order) at most 8 rows name the same one
- frontier_slot: int32 [3, 256, 16], P(None, ('rep', 'dom')), may hold values from 0 to 511
- query_tokens: bfloat16 [256, 32, 128], P(('rep', 'dom')), may hold values from -6 to 6
- passage_tiles: bfloat16 [8192, 128, 128], P('dom'), may hold values from -0.5 to 0.5
- passage_len: int32 [8192], P('dom'), may hold values from 16 to 128
- cand_owner: int32 [256, 32, 1], P(('rep', 'dom')), may hold values from 0 to 31; in each aligned block of 256 rows (0 to 255, 256 to 511, ..., all dimensions but the last counted through in order) at most 16 rows name the same one
- cand_slot: int32 [256, 32], P(('rep', 'dom')), may hold values from 0 to 255
Outputs:
- beam_scores: float32 [3, 256, 16], P(None, ('rep', 'dom'))
- maxsim_scores: float32 [256, 32], P(('rep', 'dom'))
The draws below stay inside these ranges and needn't reach their ends.
Inputs may be any that keep to these rules, and one draw needn't show every extreme that they name: `frontier_owner`: the 16 partitions of one query in one round are distinct. Among the queries of one index of dom in one round no partition is named by more than 8 queries, a bound that some block reaches. `cand_owner`: among the candidates of the queries of one index of dom no shard is named more than 16 times, a bound that some block reaches. Candidates may repeat.
All inputs are finite; a program needn't handle non-finite values.
Results may differ from the reference program's by a relative error of at most 0.0003.
Values may be sent and summed in bfloat16 or wider, within the bound.
No kernel may reach another device: no remote copies, remote signals or barrier semaphores. Data moves between devices by JAX's collectives and lax.ppermute only.
A program may use at most 256 MiB of HBM per device.

```python
import math
import jax
import jax.numpy as jnp
import numpy as np
from jax import lax

FDE = 10240
DIM = 128
QT = 32
PT = 128
ROUNDS = 3
FRONT = 16
CAND = 32
Q_DEV = 8
NODE_DEV = 512
PASS_DEV = 256
QUERIES = 256
NODES = 16384
PASSAGES = 8192
CAP_BEAM = 8
CAP_CAND = 16
N_DOM = 32


def set_ends(entries, rng, least, largest):
    longest = entries.shape.index(max(entries.shape))
    spots = []
    for shift in (0, 1):
        where = [jax.random.randint(jax.random.fold_in(rng, axis), (), 0, length) for axis, length in enumerate(entries.shape)]
        where[longest] = (where[longest] + shift) % entries.shape[longest]
        spots.append(tuple(where))
    return entries.at[spots[0]].set(least).at[spots[1]].set(largest)


def level_of(rng, extent, pieces, smallest, top_value):
    def one(dim, blocks):
        heights = jax.random.uniform(jax.random.fold_in(jax.random.fold_in(rng, 6), dim), (blocks,), jnp.float32, smallest / len(pieces), top_value / len(pieces))
        return jnp.repeat(jnp.exp(heights), extent[dim] // blocks).reshape((-1,) + (1,) * (len(extent) - dim - 1))

    factor_of = one(*pieces[0])
    for cut in pieces[1:]:
        factor_of = factor_of * one(*cut)
    return factor_of


def deal_out(key, own, number, rows, number_of, top, reach, skew):
    sequence = jax.random.permutation(key, number_of)
    heavy_load, usual = portions_of(number_of, rows * top, reach, skew, True), portions_of(number_of, rows * top, reach, skew, False)
    places = jnp.arange(number_of)

    def named(sizes, rotation):
        used = int((sizes > 0).sum())
        fixed = max(1, used // 4)
        passed = fixed + (places - fixed + rotation * (used - fixed)) % max(1, number_of - fixed)
        return jnp.zeros((number_of,), jnp.int32).at[sequence[jnp.where(places < fixed, places, passed)]].set(jnp.asarray(sizes, jnp.int32))

    sizes = jnp.where(number % 4 == 0, named(heavy_load, number // 4), named(usual, number - number // 4 - 1))
    mixed = jax.random.permutation(jax.random.fold_in(own, 3), number_of)
    giver, receiver = mixed[0:number_of // 2 * 2:2], mixed[1:number_of // 2 * 2:2]
    slack = jnp.minimum(sizes[giver] - 1, reach - sizes[receiver]) // 2
    slack = jnp.where((giver == sequence[0]) | (receiver == sequence[0]) | (sizes[receiver] == 0), 0, jnp.maximum(slack, 0))
    passed = jax.random.randint(jax.random.fold_in(own, 4), (number_of // 2,), 0, 1 << 20) % (slack + 1)
    sizes = sizes.at[giver].add(-passed).at[receiver].add(passed)
    labels = jnp.searchsorted(jnp.cumsum(sizes), jnp.arange(rows * top), side="right").astype(jnp.int32)
    listing = labels.reshape(top, rows).T
    listing = listing[jax.random.permutation(jax.random.fold_in(own, 1), rows)]
    rotation = jax.random.randint(jax.random.fold_in(own, 2), (rows, 1), 0, top)
    return jnp.take_along_axis(listing, (jnp.arange(top)[None, :] + rotation) % top, axis=1)


def portions_of(number_of, total, bound, slope, full):
    portions = [(1 << 20) // math.isqrt(rank ** slope) + 1 for rank in range(1, number_of + 1)]
    largest = bound if full else min(bound, max(-(-total // number_of), total * portions[0] // sum(portions)))
    least = 1 if total - largest >= number_of - 1 else 0
    counts, surplus = [largest] + [least] * (number_of - 1), total - largest - least * (number_of - 1)
    while surplus > 0:
        candidates = [i for i in range(1, number_of) if counts[i] < largest] or [i for i in range(1, number_of) if counts[i] < bound]
        whole, left = sum([portions[i] for i in candidates]), surplus
        for i in candidates:
            extra = min(bound - counts[i], max(1, left * portions[i] // whole), surplus)
            counts[i] = counts[i] + extra
            surplus = surplus - extra
    return np.array(counts)


def bell_draw(stream_key, shape, width, limit, pieces=(), kind=jnp.bfloat16):
    level = level_of(stream_key, shape, pieces, -0.22, 0.18) if pieces else 1.0
    result = jax.random.normal(stream_key, shape, jnp.float32) * width * level
    return jnp.minimum(jnp.maximum(result, -limit), limit).astype(kind)


def setup_inputs(seed: int = 0, part: int = 0) -> dict:
    seeds = jax.random.split(jax.random.key(seed), 10)
    part_splits = jax.random.split(jax.random.fold_in(seeds[9], part), 10)
    query_fde = bell_draw(part_splits[0], (QUERIES, FDE), 1.0, 6.0, ((0, 32),))
    doc_fde = bell_draw(seeds[1], (NODES, FDE), FDE ** -0.5, 0.0625, ((0, 32),))
    frontier_owner_keys = jax.random.split(jax.random.fold_in(part_splits[2], 1), ROUNDS * QUERIES // Q_DEV)
    frontier_owner_turns = jax.random.permutation(jax.random.fold_in(part_splits[2], 3), ROUNDS * QUERIES // Q_DEV)
    frontier_owner = jax.vmap(lambda own, number: deal_out(jax.random.fold_in(part_splits[2], 2), own, number, Q_DEV, N_DOM, FRONT, CAP_BEAM, 2))(frontier_owner_keys, frontier_owner_turns).reshape((ROUNDS, QUERIES, FRONT))
    frontier_slot = set_ends(jax.random.randint(part_splits[3], (ROUNDS, QUERIES, FRONT), 0, NODE_DEV), jax.random.fold_in(part_splits[3], 1), 0, NODE_DEV - 1).astype(jnp.int32)
    query_tokens = bell_draw(part_splits[4], (QUERIES, QT, DIM), 1.0, 6.0, ((0, 32),))
    passage_tiles = bell_draw(seeds[5], (PASSAGES, PT, DIM), DIM ** -0.5, 0.5, ((0, 32),))
    passage_len = set_ends(jax.random.randint(seeds[6], (PASSAGES,), max(1, PT // 8), PT + 1), jax.random.fold_in(seeds[6], 1), max(1, PT // 8), PT).astype(jnp.int32)
    cand_owner_keys = jax.random.split(jax.random.fold_in(part_splits[7], 1), QUERIES * CAND // (Q_DEV * CAND))
    cand_owner_turns = jax.random.permutation(jax.random.fold_in(part_splits[7], 3), QUERIES * CAND // (Q_DEV * CAND))
    cand_owner = jax.vmap(lambda own, number: deal_out(jax.random.fold_in(part_splits[7], 2), own, number, Q_DEV * CAND, N_DOM, 1, CAP_CAND, 2))(cand_owner_keys, cand_owner_turns).reshape((QUERIES, CAND, 1))
    cand_slot = set_ends(jax.random.randint(part_splits[8], (QUERIES, CAND), 0, PASS_DEV), jax.random.fold_in(part_splits[8], 1), 0, PASS_DEV - 1).astype(jnp.int32)
    return dict(query_fde=query_fde, doc_fde=doc_fde, frontier_owner=frontier_owner, frontier_slot=frontier_slot, query_tokens=query_tokens, passage_tiles=passage_tiles, passage_len=passage_len, cand_owner=cand_owner, cand_slot=cand_slot)


masked_value = -1e30


def pair_scores(tokens, tile_data, lengths):
    similarity = jnp.einsum("qd,ktd->kqt", tokens.astype(jnp.float32), tile_data.astype(jnp.float32), precision=lax.Precision.HIGHEST)
    is_valid = jnp.arange(tile_data.shape[1], dtype=jnp.int32)[None, None, :] < lengths[:, None, None]
    maxima = jnp.max(jnp.where(is_valid, similarity, masked_value), axis=2)
    return jnp.mean(maxima, axis=1)


def reference(query_fde, doc_fde, frontier_owner, frontier_slot, query_tokens, passage_tiles, passage_len, cand_owner, cand_slot):
    def one_round(inputs):
        owners, slot_ids = inputs
        node_ids = (owners * NODE_DEV + slot_ids).astype(jnp.int32)
        fde_rows = doc_fde[node_ids]
        return jnp.einsum("qf,qkf->qk", query_fde.astype(jnp.float32), fde_rows.astype(jnp.float32), precision=lax.Precision.HIGHEST)

    beam_scores = lax.map(one_round, (frontier_owner, frontier_slot))

    def one_query(inputs):
        tokens, owners, slot_ids = inputs
        tile_ids = (owners[:, 0] * PASS_DEV + slot_ids).astype(jnp.int32)
        return pair_scores(tokens, passage_tiles[tile_ids], passage_len[tile_ids])

    maxsim_scores = lax.map(one_query, (query_tokens, cand_owner, cand_slot))
    return beam_scores, maxsim_scores
```

```python
import functools
import math

import jax
import jax.numpy as jnp
from jax import lax
from jax.experimental import pallas as pl
from jax.experimental.pallas import tpu as pltpu
from jax.sharding import PartitionSpec as P

masked_value = -1e30
LANES = 128
GROUP = 4
VMEM = pl.BlockSpec(memory_space=pltpu.VMEM)
NT = (((1,), (1,)), ((), ()))


def sources_of(order):
    masks = [0]
    for bit in order:
        masks = masks + [m ^ bit for m in masks]
    return masks


def orders_of(n):
    bits = [1 << i for i in range(1, n.bit_length() - 1)]
    far, rest = bits[-1], bits[:-1]
    return [[far] + rest[i:] + rest[:i] for i in (0, len(rest) - 1, 1)]


def exchange(x, bit, n):
    return lax.ppermute(x, "dom", [(i, i ^ bit) for i in range(n)])


def place(values, offset):
    w = values.shape[1]
    where = lax.broadcasted_iota(jnp.int32, (w, LANES), 0) + offset
    lane = lax.broadcasted_iota(jnp.int32, (w, LANES), 1)
    return jnp.dot(
        values.astype(jnp.float32).astype(jnp.bfloat16),
        (where == lane).astype(jnp.float32).astype(jnp.bfloat16),
        preferred_element_type=jnp.float32,
    )


def prep_kernel(parts, fo, fs, co, cs, tok, out):
    rounds, _, front = fo.shape
    rows = tok.shape[0]
    cand_at = rounds * front
    first = place(co[...] * parts, cand_at)
    second = place(cs[...], cand_at)
    for r in range(rounds):
        first = first + place(fo[r] * parts + (fs[r] >> 8), r * front)
        second = second + place(fs[r] & 255, r * front)
    out[:rows, :] = tok[...]
    out[rows:, :] = jnp.concatenate([first, second], axis=0).astype(jnp.bfloat16)


def maxsim_kernel(cand_at, cands, stride, lst, cnt, lens, own, other, tiles, out):
    qt = (stride - 16) // 8
    blocks = own.shape[0] // stride
    pt = tiles.shape[1]
    cap = lst.shape[0] // (2 * blocks)
    width = stride - 16
    token = lax.broadcasted_iota(jnp.int32, (pt, width), 0)
    column = lax.broadcasted_iota(jnp.int32, (1, width), 1) // qt
    row = lax.broadcasted_iota(jnp.int32, (8, LANES), 0)
    lane = lax.broadcasted_iota(jnp.int32, (8, LANES), 1)
    for side, ref in enumerate((own, other)):

        def source(b, carry, side=side, ref=ref):
            at = side * blocks + b
            weights = ref[pl.ds(pl.multiple_of(b * stride, 16), width), :]
            held = cnt[at]

            def group(g, acc):
                entries = [lst[at * cap + g * GROUP + j] for j in range(GROUP)]
                slots = [e & 255 for e in entries]
                data = jnp.concatenate([tiles[s] for s in slots], axis=0)
                sim = lax.dot_general(data, weights, NT, preferred_element_type=jnp.float32)
                for j in range(GROUP):
                    pair = entries[j] >> 8
                    query, cand = pair // cands, pair % cands
                    part = sim[j * pt : (j + 1) * pt, :]
                    part = jnp.where(token < lens[slots[j]], part, masked_value)
                    top = jnp.max(part, axis=0, keepdims=True)
                    score = jnp.sum(jnp.where(column == query, top, 0.0), axis=1, keepdims=True) * (1.0 / qt)
                    there = jnp.where(g * GROUP + j < held, cand_at + cand, -1)
                    acc = acc + jnp.where((row == query) & (lane == there), score, 0.0)
                return acc

            out[at] = lax.fori_loop(0, (held + GROUP - 1) // GROUP, group, jnp.zeros((8, LANES), jnp.float32))
            return carry

        lax.fori_loop(0, blocks, source, 0)


def beam_kernel(own, other, doc, total):
    @pl.when(pl.program_id(0) == 0)
    def _():
        total[...] = jnp.zeros_like(total)

    left = jnp.concatenate([own[...], other[...]], axis=0)
    total[...] += lax.dot_general(left, doc[...], NT, preferred_element_type=jnp.float32)


def last_kernel(cfg, me_ref, own, other, doc, so_far, codes_own, codes_other, maxsim, out, total):
    order, first_order, code_order, parts, cand_at, stride = cfg
    blocks = len(order)
    half = blocks * 8

    @pl.when(pl.program_id(0) == 0)
    def _():
        for side in range(2):
            for p in range(blocks):
                q = first_order.index(order[p])
                total[side * half + p * 8 : side * half + p * 8 + 8, :] = so_far[
                    side * half + q * 8 : side * half + q * 8 + 8, :
                ]

    left = jnp.concatenate([own[...], other[...]], axis=0)
    total[...] += lax.dot_general(left, doc[...], NT, preferred_element_type=jnp.float32)

    @pl.when(pl.program_id(0) == pl.num_programs(0) - 1)
    def _():
        me = me_ref[0]
        lane = lax.broadcasted_iota(jnp.int32, (8, LANES), 1)
        nodes = total.shape[1]
        for side, ref in enumerate((codes_own, codes_other)):
            for p in range(blocks):
                t = code_order.index(order[p])
                codes = ref[t * stride + stride - 16 : (t + 1) * stride, :].astype(jnp.float32).astype(jnp.int32)
                owner, high, low = codes[:8] // parts, codes[:8] % parts, codes[8:]
                slot = high * 256 + low
                within, page = slot % LANES, slot // LANES
                rows = total[side * half + p * 8 : side * half + p * 8 + 8, :]
                found = jnp.zeros((8, LANES), jnp.float32)
                for g in range(nodes // LANES):
                    here = jnp.take_along_axis(rows[:, g * LANES : (g + 1) * LANES], within, axis=1)
                    found = jnp.where(page == g, here, found)
                found = jnp.where(owner == me, found, 0.0)
                out[me ^ (order[p] + side)] = jnp.where(lane < cand_at, found, maxsim[side * blocks + t])


def sum_kernel(rounds, front, cands, parts, beam, maxsim):
    total = parts[0]
    for i in range(1, parts.shape[0]):
        total = total + parts[i]
    for r in range(rounds):
        beam[r] = (total if r == 0 else pltpu.roll(total, LANES - r * front, axis=1))[:, :front]
    maxsim[...] = pltpu.roll(total, LANES - rounds * front, axis=1)[:, :cands]


def local(n, query_fde, doc_fde, frontier_owner, frontier_slot, query_tokens, passage_tiles, passage_len, cand_owner, cand_slot):
    rounds, queries, front = frontier_owner.shape
    cands = cand_slot.shape[1]
    nodes, fde = doc_fde.shape
    qt, dim = query_tokens.shape[1:]
    parts = nodes // 256
    cand_at = rounds * front
    assert n & (n - 1) == 0 and queries == 8 and dim == LANES and nodes % 256 == 0
    assert cand_at + cands <= LANES and n * parts <= 256 and passage_tiles.shape[0] <= 256
    me = lax.axis_index("dom").astype(jnp.int32)
    stride = queries * qt + 16
    blocks = n // 2
    orders = orders_of(n)
    masks = [sources_of(o) for o in orders]

    packed = pl.pallas_call(
        functools.partial(prep_kernel, parts),
        out_shape=jax.ShapeDtypeStruct((stride, dim), jnp.bfloat16),
        in_specs=[VMEM] * 5,
        out_specs=VMEM,
        name="pack",
    )(frontier_owner, frontier_slot, cand_owner.reshape(queries, cands), cand_slot, query_tokens.reshape(queries * qt, dim))

    half = fde // 2
    chunks = [packed, query_fde[:, :half], query_fde[:, half:]]
    for step in range(len(orders[0])):
        for k in range(3):
            chunks[k] = jnp.concatenate([chunks[k], exchange(chunks[k], orders[k][step], n)], axis=0)
    pairs = [(c, exchange(c, 1, n)) for c in chunks]
    (tok_own, tok_other), (a_own, a_other), (b_own, b_other) = pairs

    codes = jnp.stack(pairs[0]).reshape(n, stride, dim)[:, queries * qt :, cand_at : cand_at + cands]
    codes = codes.astype(jnp.int32)
    mine = (codes[:, :queries] // parts == me).reshape(n, queries * cands)
    slots = codes[:, queries:].reshape(n, queries * cands)
    cap = max(2, min(queries * cands, 2 * queries * cands // n))
    position = jnp.cumsum(mine.astype(jnp.int32), axis=1) - 1
    payload = jnp.arange(queries * cands, dtype=jnp.int32)[None] * 256 + slots
    chosen = mine[:, None, :] & (position[:, None, :] == jnp.arange(cap, dtype=jnp.int32)[None, :, None])
    entries = jnp.sum(jnp.where(chosen, payload[:, None, :], 0), axis=2)
    counts = jnp.sum(mine.astype(jnp.int32), axis=1)

    pairs_bound = n * cap
    maxsim = pl.pallas_call(
        functools.partial(maxsim_kernel, cand_at, cands, stride),
        out_shape=jax.ShapeDtypeStruct((n, 8, LANES), jnp.float32),
        grid_spec=pltpu.PrefetchScalarGridSpec(
            num_scalar_prefetch=3, grid=(), in_specs=[VMEM] * 3, out_specs=VMEM
        ),
        compiler_params=pltpu.CompilerParams(vmem_limit_bytes=24 << 20),
        cost_estimate=pl.CostEstimate(
            flops=2 * pairs_bound * 128 * 256 * 128, bytes_accessed=8 << 20, transcendentals=0
        ),
        name="maxsim",
    )(entries.reshape(-1), counts, passage_len, tok_own, tok_other, passage_tiles)

    block = math.gcd(half, 1280)
    steps = half // block
    rows = n * 8

    def beam_specs(first, prefetch):
        left = pl.BlockSpec((rows // 2, block), lambda i, *_: (0, i))
        return [left, left, pl.BlockSpec((nodes, block), lambda i, *_: (0, first + i))]

    whole = pl.BlockSpec((rows, nodes), lambda i, *_: (0, 0))
    cost = pl.CostEstimate(flops=2 * rows * nodes * half, bytes_accessed=2 * (rows + nodes) * half, transcendentals=0)
    so_far = pl.pallas_call(
        beam_kernel,
        out_shape=jax.ShapeDtypeStruct((rows, nodes), jnp.float32),
        grid=(steps,),
        in_specs=beam_specs(0, 0),
        out_specs=whole,
        compiler_params=pltpu.CompilerParams(vmem_limit_bytes=16 << 20),
        cost_estimate=cost,
        name="beam",
    )(a_own, a_other, doc_fde)
    cfg = (masks[2], masks[1], masks[0], parts, cand_at, stride)
    full = lambda shape: pl.BlockSpec(shape, lambda i, *_: (0,) * len(shape))
    scored = pl.pallas_call(
        functools.partial(last_kernel, cfg),
        out_shape=jax.ShapeDtypeStruct((n, 8, LANES), jnp.float32),
        grid_spec=pltpu.PrefetchScalarGridSpec(
            num_scalar_prefetch=1,
            grid=(steps,),
            in_specs=beam_specs(steps, 1)
            + [whole, full(tok_own.shape), full(tok_own.shape), full((n, 8, LANES))],
            out_specs=full((n, 8, LANES)),
            scratch_shapes=[pltpu.VMEM((rows, nodes), jnp.float32)],
        ),
        compiler_params=pltpu.CompilerParams(vmem_limit_bytes=24 << 20),
        cost_estimate=cost,
        name="beam_last",
    )(me.reshape(1), b_own, b_other, doc_fde, so_far, tok_own, tok_other, maxsim)

    returned = lax.all_to_all(scored, "dom", split_axis=0, concat_axis=0, tiled=True)
    return pl.pallas_call(
        functools.partial(sum_kernel, rounds, front, cands),
        out_shape=(
            jax.ShapeDtypeStruct((rounds, queries, front), jnp.float32),
            jax.ShapeDtypeStruct((queries, cands), jnp.float32),
        ),
        in_specs=[VMEM],
        out_specs=(VMEM, VMEM),
        name="collect",
    )(returned)


def solution(mesh):
    in_specs = (
        P(("rep", "dom"), None),
        P("dom", None),
        P(None, ("rep", "dom"), None),
        P(None, ("rep", "dom"), None),
        P(("rep", "dom"), None, None),
        P("dom", None, None),
        P("dom"),
        P(("rep", "dom"), None, None),
        P(("rep", "dom"), None),
    )
    out_specs = (P(None, ("rep", "dom"), None), P(("rep", "dom"), None))
    return jax.shard_map(
        functools.partial(local, mesh.shape["dom"]), mesh=mesh, in_specs=in_specs, out_specs=out_specs, check_vma=False
    )
```

```python
import functools
import math

import jax
import jax.numpy as jnp
from jax import lax
from jax.experimental import pallas as pl
from jax.experimental.pallas import tpu as pltpu
from jax.sharding import PartitionSpec as P

masked_value = -1e30
LANES = 128
VMEM = pl.BlockSpec(memory_space=pltpu.VMEM)
NT = (((1,), (1,)), ((), ()))


def sources_of(order):
    masks = [0]
    for bit in order:
        masks = masks + [m ^ bit for m in masks]
    return masks


def orders_of(n):
    bits = [1 << i for i in range(1, n.bit_length() - 1)]
    far, rest = bits[-1], bits[:-1]
    return [[far] + rest[i:] + rest[:i] for i in (0, len(rest) - 1, 1)]


def exchange(x, bit, n):
    return lax.ppermute(x, "dom", [(i, i ^ bit) for i in range(n)])


def place(values, offset):
    w = values.shape[1]
    where = lax.broadcasted_iota(jnp.int32, (w, LANES), 0) + offset
    lane = lax.broadcasted_iota(jnp.int32, (w, LANES), 1)
    return jnp.dot(
        values.astype(jnp.float32).astype(jnp.bfloat16),
        (where == lane).astype(jnp.float32).astype(jnp.bfloat16),
        preferred_element_type=jnp.float32,
    )


def ids(shape, axis):
    return lax.broadcasted_iota(jnp.int32, shape, axis)


def exact(values):
    return values.astype(jnp.float32).astype(jnp.bfloat16)


def pick(a, b):
    return jnp.dot(exact(a), exact(b), preferred_element_type=jnp.float32)


def prep_kernel(parts, slots, cap, fo, fs, co, cs, tok, out):
    rounds, queries, front = fo.shape
    rows, cands = tok.shape[0], co.shape[1]
    pairs = queries * cands
    low_at = rounds * front
    codes = jnp.zeros((queries, LANES), jnp.float32)
    for r in range(rounds):
        codes = codes + place(fo[r] * parts + (fs[r] >> 8), r * front)
        codes = codes + place(fs[r] & 255, low_at + r * front)

    across = (ids((cands, pairs), 1) % cands == ids((cands, pairs), 0))
    mine = ids((queries, pairs), 1) // cands == ids((queries, pairs), 0)
    line = lambda v: jnp.sum(jnp.where(mine, pick(v, across), 0.0), axis=0, keepdims=True)
    owner_line, slot_line = line(co[...]), line(cs[...])
    down = ids((pairs, queries), 0) // cands == ids((pairs, queries), 1)
    here = ids((pairs, cands), 0) % cands == ids((pairs, cands), 1)
    owner = jnp.sum(jnp.where(here, pick(down, co[...]), 0.0), axis=1, keepdims=True)
    earlier = (owner == owner_line) & (ids((pairs, pairs), 1) < ids((pairs, pairs), 0))
    position = jnp.sum(jnp.where(earlier, 1.0, 0.0), axis=1, keepdims=True)
    target = (owner * cap + position).astype(jnp.int32)
    number = (ids((1, pairs), 1) + 1).astype(jnp.float32)
    table = jnp.zeros((8, LANES), jnp.float32)
    for g in range(slots // LANES):
        row = ids((8, pairs), 0)
        values = jnp.where(row == 2 * g, number, jnp.where(row == 2 * g + 1, slot_line, 0.0))
        table = table + pick(values, target == ids((pairs, LANES), 1) + g * LANES)
    out[:rows, :] = tok[...]
    out[rows:, :] = jnp.concatenate([codes, table], axis=0).astype(jnp.bfloat16)


def maxsim_kernel(cand_at, cands, cap, me_ref, lens, own, other, tiles, out, listed, lst, sem):
    blocks = out.shape[0] // 2
    stride = own.shape[0] // blocks
    pt = tiles.shape[1]
    qt = (stride - 16) // 8
    start = me_ref[0] * cap
    row, lane = ids((8, LANES), 0), ids((8, LANES), 1)
    group = start // LANES
    for side, ref in enumerate((own, other)):
        for b in range(blocks):
            table = ref[(b + 1) * stride - 16 : (b + 1) * stride, :].astype(jnp.float32)[8:]
            weight = jnp.where(row == 2 * group, 256.0, jnp.where(row == 2 * group + 1, 1.0, 0.0))
            at = side * blocks + b
            listed[at : at + 1, :] = jnp.sum(table * weight, axis=0, keepdims=True).astype(jnp.int32)
    listed[...] = pltpu.roll(listed[...], lax.rem(LANES - start % LANES, LANES), axis=1)
    copy = pltpu.make_async_copy(listed, lst, sem)
    copy.start()
    copy.wait()

    spot = jnp.where((lane >= cand_at) & (lane < cand_at + cands), row * cands + lane - cand_at, -1)
    token = ids((pt, qt), 0)

    def score(ref, b, at):
        tops, pairs = [], []
        for k in range(cap):
            entry = lst[at, k]
            slot, pair = entry & 255, (entry >> 8) - 1
            query = jnp.maximum(pair, 0) // cands
            tokens = ref[pl.ds(pl.multiple_of(b * stride + query * qt, 16), qt), :]
            sim = lax.dot_general(tiles[slot], tokens, NT, preferred_element_type=jnp.float32)
            sim = jnp.where(token < lens[slot], sim, masked_value)
            tops.append(jnp.max(sim, axis=0, keepdims=True))
            pairs.append(jnp.where(pair < 0, -2, pair))
        means = jnp.sum(jnp.concatenate(tops, axis=0), axis=1, keepdims=True) * (1.0 / qt)
        acc = jnp.zeros((8, LANES), jnp.float32)
        for k in range(cap):
            acc = acc + jnp.where(spot == pairs[k], means[k : k + 1, :], 0.0)
        out[at] = acc

    def step(i, carry):
        for u in range(2):
            score(own, 2 * i + u, 2 * i + u)
            score(other, 2 * i + u, blocks + 2 * i + u)
        return carry

    lax.fori_loop(0, blocks // 2, step, 0)


def beam_kernel(own, other, doc, total):
    @pl.when(pl.program_id(0) == 0)
    def _():
        total[...] = jnp.zeros_like(total)

    left = jnp.concatenate([own[...], other[...]], axis=0)
    total[...] += lax.dot_general(left, doc[...], NT, preferred_element_type=jnp.float32)


def last_kernel(cfg, me_ref, own, other, doc, so_far, codes_own, codes_other, maxsim, out, total):
    order, first_order, code_order, parts, cand_at, stride = cfg
    blocks = len(order)
    half = blocks * 8

    @pl.when(pl.program_id(0) == 0)
    def _():
        for side in range(2):
            for p in range(blocks):
                q = first_order.index(order[p])
                total[side * half + p * 8 : side * half + p * 8 + 8, :] = so_far[
                    side * half + q * 8 : side * half + q * 8 + 8, :
                ]

    left = jnp.concatenate([own[...], other[...]], axis=0)
    total[...] += lax.dot_general(left, doc[...], NT, preferred_element_type=jnp.float32)

    @pl.when(pl.program_id(0) == pl.num_programs(0) - 1)
    def _():
        me = me_ref[0]
        lane = lax.broadcasted_iota(jnp.int32, (8, LANES), 1)
        nodes = total.shape[1]
        for side, ref in enumerate((codes_own, codes_other)):
            for p in range(blocks):
                t = code_order.index(order[p])
                codes = ref[(t + 1) * stride - 16 : (t + 1) * stride, :].astype(jnp.float32)[:8]
                low = pltpu.roll(codes, LANES - cand_at, axis=1).astype(jnp.int32)
                codes = codes.astype(jnp.int32)
                owner, high = codes // parts, codes % parts
                slot = high * 256 + low
                within, page = slot % LANES, slot // LANES
                rows = total[side * half + p * 8 : side * half + p * 8 + 8, :]
                found = jnp.zeros((8, LANES), jnp.float32)
                for g in range(nodes // LANES):
                    here = jnp.take_along_axis(rows[:, g * LANES : (g + 1) * LANES], within, axis=1)
                    found = jnp.where(page == g, here, found)
                found = jnp.where(owner == me, found, 0.0)
                out[me ^ (order[p] + side)] = jnp.where(lane < cand_at, found, maxsim[side * blocks + t])


def sum_kernel(rounds, front, cands, parts, beam, maxsim):
    total = parts[0]
    for i in range(1, parts.shape[0]):
        total = total + parts[i]
    for r in range(rounds):
        beam[r] = (total if r == 0 else pltpu.roll(total, LANES - r * front, axis=1))[:, :front]
    maxsim[...] = pltpu.roll(total, LANES - rounds * front, axis=1)[:, :cands]


def local(n, query_fde, doc_fde, frontier_owner, frontier_slot, query_tokens, passage_tiles, passage_len, cand_owner, cand_slot):
    rounds, queries, front = frontier_owner.shape
    cands = cand_slot.shape[1]
    nodes, fde = doc_fde.shape
    qt, dim = query_tokens.shape[1:]
    parts = nodes // 256
    cand_at = rounds * front
    assert n & (n - 1) == 0 and queries == 8 and dim == LANES and nodes % 256 == 0
    assert cand_at + max(cand_at, cands) <= LANES and n * parts <= 256 and passage_tiles.shape[0] <= 256
    me = lax.axis_index("dom").astype(jnp.int32)
    stride = queries * qt + 16
    blocks = n // 2
    orders = orders_of(n)
    masks = [sources_of(o) for o in orders]

    pairs_count = queries * cands
    cap = max(2, min(pairs_count, 2 * pairs_count // n))
    slots = n * cap
    assert slots % LANES == 0 and slots <= 4 * LANES and LANES % cap == 0 and pairs_count <= 256
    packed = pl.pallas_call(
        functools.partial(prep_kernel, parts, slots, cap),
        out_shape=jax.ShapeDtypeStruct((stride, dim), jnp.bfloat16),
        in_specs=[VMEM] * 5,
        out_specs=VMEM,
        name="pack",
    )(frontier_owner, frontier_slot, cand_owner.reshape(queries, cands), cand_slot, query_tokens.reshape(queries * qt, dim))
    half = fde // 2
    chunks = [packed, query_fde[:, :half], query_fde[:, half:]]
    for step in range(len(orders[0])):
        for k in range(3):
            chunks[k] = jnp.concatenate([chunks[k], exchange(chunks[k], orders[k][step], n)], axis=0)
    pairs = [(c, exchange(c, 1, n)) for c in chunks]
    (tok_own, tok_other), (a_own, a_other), (b_own, b_other) = pairs

    pt = passage_tiles.shape[1]
    maxsim = pl.pallas_call(
        functools.partial(maxsim_kernel, cand_at, cands, cap),
        out_shape=jax.ShapeDtypeStruct((n, 8, LANES), jnp.float32),
        grid_spec=pltpu.PrefetchScalarGridSpec(
            num_scalar_prefetch=2,
            grid=(),
            in_specs=[VMEM] * 3,
            out_specs=VMEM,
            scratch_shapes=[pltpu.VMEM((n, LANES), jnp.int32), pltpu.SMEM((n, LANES), jnp.int32), pltpu.SemaphoreType.DMA],
        ),
        compiler_params=pltpu.CompilerParams(vmem_limit_bytes=16 << 20),
        cost_estimate=pl.CostEstimate(
            flops=16 * slots * pt * qt * dim, bytes_accessed=8 << 20, transcendentals=0
        ),
        name="maxsim",
    )(me.reshape(1), passage_len, tok_own, tok_other, passage_tiles)

    block = math.gcd(half, 1280)
    steps = half // block
    rows = n * 8

    def beam_specs(first, prefetch):
        left = pl.BlockSpec((rows // 2, block), lambda i, *_: (0, i))
        return [left, left, pl.BlockSpec((nodes, block), lambda i, *_: (0, first + i))]

    whole = pl.BlockSpec((rows, nodes), lambda i, *_: (0, 0))
    cost = pl.CostEstimate(flops=2 * rows * nodes * half, bytes_accessed=2 * (rows + nodes) * half, transcendentals=0)
    so_far = pl.pallas_call(
        beam_kernel,
        out_shape=jax.ShapeDtypeStruct((rows, nodes), jnp.float32),
        grid=(steps,),
        in_specs=beam_specs(0, 0),
        out_specs=whole,
        compiler_params=pltpu.CompilerParams(vmem_limit_bytes=16 << 20),
        cost_estimate=cost,
        name="beam",
    )(a_own, a_other, doc_fde)
    cfg = (masks[2], masks[1], masks[0], parts, cand_at, stride)
    full = lambda shape: pl.BlockSpec(shape, lambda i, *_: (0,) * len(shape))
    scored = pl.pallas_call(
        functools.partial(last_kernel, cfg),
        out_shape=jax.ShapeDtypeStruct((n, 8, LANES), jnp.float32),
        grid_spec=pltpu.PrefetchScalarGridSpec(
            num_scalar_prefetch=1,
            grid=(steps,),
            in_specs=beam_specs(steps, 1)
            + [whole, full(tok_own.shape), full(tok_own.shape), full((n, 8, LANES))],
            out_specs=full((n, 8, LANES)),
            scratch_shapes=[pltpu.VMEM((rows, nodes), jnp.float32)],
        ),
        compiler_params=pltpu.CompilerParams(vmem_limit_bytes=24 << 20),
        cost_estimate=cost,
        name="beam_last",
    )(me.reshape(1), b_own, b_other, doc_fde, so_far, tok_own, tok_other, maxsim)

    returned = lax.all_to_all(scored, "dom", split_axis=0, concat_axis=0, tiled=True)
    return pl.pallas_call(
        functools.partial(sum_kernel, rounds, front, cands),
        out_shape=(
            jax.ShapeDtypeStruct((rounds, queries, front), jnp.float32),
            jax.ShapeDtypeStruct((queries, cands), jnp.float32),
        ),
        in_specs=[VMEM],
        out_specs=(VMEM, VMEM),
        name="collect",
    )(returned)


def solution(mesh):
    in_specs = (
        P(("rep", "dom"), None),
        P("dom", None),
        P(None, ("rep", "dom"), None),
        P(None, ("rep", "dom"), None),
        P(("rep", "dom"), None, None),
        P("dom", None, None),
        P("dom"),
        P(("rep", "dom"), None, None),
        P(("rep", "dom"), None),
    )
    out_specs = (P(None, ("rep", "dom"), None), P(("rep", "dom"), None))
    return jax.shard_map(
        functools.partial(local, mesh.shape["dom"]), mesh=mesh, in_specs=in_specs, out_specs=out_specs, check_vma=False
    )
```

```python
import functools
import math

import jax
import jax.numpy as jnp
from jax import lax
from jax.experimental import pallas as pl
from jax.experimental.pallas import tpu as pltpu
from jax.sharding import PartitionSpec as P

masked_value = -1e30
LANES = 128
VMEM = pl.BlockSpec(memory_space=pltpu.VMEM)
NT = (((1,), (1,)), ((), ()))


def sources_of(order):
    masks = [0]
    for bit in order:
        masks = masks + [m ^ bit for m in masks]
    return masks


def orders_of(n):
    bits = [1 << i for i in range(1, n.bit_length() - 1)]
    far, rest = bits[-1:], bits[:-1]
    return [[16, 2, 4, 8], [16, 8, 2, 4], [16, 4, 8, 2]]


TIES = {}


def exchange(x, bit, n):
    return lax.ppermute(x, "dom", [(i, i ^ bit) for i in range(n)])


def place(values, offset):
    w = values.shape[1]
    where = lax.broadcasted_iota(jnp.int32, (w, LANES), 0) + offset
    lane = lax.broadcasted_iota(jnp.int32, (w, LANES), 1)
    return jnp.dot(
        values.astype(jnp.float32).astype(jnp.bfloat16),
        (where == lane).astype(jnp.float32).astype(jnp.bfloat16),
        preferred_element_type=jnp.float32,
    )


def ids(shape, axis):
    return lax.broadcasted_iota(jnp.int32, shape, axis)


def exact(values):
    return values.astype(jnp.float32).astype(jnp.bfloat16)


def pick(a, b):
    return jnp.dot(exact(a), exact(b), preferred_element_type=jnp.float32)


def prep_kernel(parts, slots, cap, fo, fs, co, cs, tok, out):
    rounds, queries, front = fo.shape
    rows, cands = tok.shape[0], co.shape[1]
    pairs = queries * cands
    low_at = rounds * front
    codes = jnp.zeros((queries, LANES), jnp.float32)
    for r in range(rounds):
        codes = codes + place(fo[r] * parts + (fs[r] >> 8), r * front)
        codes = codes + place(fs[r] & 255, low_at + r * front)

    across = (ids((cands, pairs), 1) % cands == ids((cands, pairs), 0))
    mine = ids((queries, pairs), 1) // cands == ids((queries, pairs), 0)
    line = lambda v: jnp.sum(jnp.where(mine, pick(v, across), 0.0), axis=0, keepdims=True)
    owner_line, slot_line = line(co[...]), line(cs[...])
    down = ids((pairs, queries), 0) // cands == ids((pairs, queries), 1)
    here = ids((pairs, cands), 0) % cands == ids((pairs, cands), 1)
    owner = jnp.sum(jnp.where(here, pick(down, co[...]), 0.0), axis=1, keepdims=True)
    earlier = (owner == owner_line) & (ids((pairs, pairs), 1) < ids((pairs, pairs), 0))
    position = jnp.sum(jnp.where(earlier, 1.0, 0.0), axis=1, keepdims=True)
    target = (owner * cap + position).astype(jnp.int32)
    number = (ids((1, pairs), 1) + 1).astype(jnp.float32)
    table = jnp.zeros((8, LANES), jnp.float32)
    for g in range(slots // LANES):
        row = ids((8, pairs), 0)
        values = jnp.where(row == 2 * g, number, jnp.where(row == 2 * g + 1, slot_line, 0.0))
        table = table + pick(values, target == ids((pairs, LANES), 1) + g * LANES)
    out[:rows, :] = tok[...]
    out[rows:, :] = jnp.concatenate([codes, table], axis=0).astype(jnp.bfloat16)


def maxsim_kernel(cand_at, cands, cap, me_ref, lens, own, other, tiles, out, listed, lst, sem):
    blocks = out.shape[0] // 2
    stride = own.shape[0] // blocks
    pt = tiles.shape[1]
    qt = (stride - 16) // 8
    start = me_ref[0] * cap
    row, lane = ids((8, LANES), 0), ids((8, LANES), 1)
    group = start // LANES
    for side, ref in enumerate((own, other)):
        for b in range(blocks):
            table = ref[(b + 1) * stride - 16 : (b + 1) * stride, :].astype(jnp.float32)[8:]
            weight = jnp.where(row == 2 * group, 256.0, jnp.where(row == 2 * group + 1, 1.0, 0.0))
            at = side * blocks + b
            listed[at : at + 1, :] = jnp.sum(table * weight, axis=0, keepdims=True).astype(jnp.int32)
    listed[...] = pltpu.roll(listed[...], lax.rem(LANES - start % LANES, LANES), axis=1)
    copy = pltpu.make_async_copy(listed, lst, sem)
    copy.start()
    copy.wait()

    spot = jnp.where((lane >= cand_at) & (lane < cand_at + cands), row * cands + lane - cand_at, -1)
    token = ids((pt, qt), 0)

    def score(ref, b, at):
        tops, pairs = [], []
        for k in range(cap):
            entry = lst[at, k]
            slot, pair = entry & 255, (entry >> 8) - 1
            query = jnp.maximum(pair, 0) // cands
            tokens = ref[pl.ds(pl.multiple_of(b * stride + query * qt, 16), qt), :]
            sim = lax.dot_general(tiles[slot], tokens, NT, preferred_element_type=jnp.float32)
            sim = jnp.where(token < lens[slot], sim, masked_value)
            tops.append(jnp.max(sim, axis=0, keepdims=True))
            pairs.append(jnp.where(pair < 0, -2, pair))
        means = jnp.sum(jnp.concatenate(tops, axis=0), axis=1, keepdims=True) * (1.0 / qt)
        acc = jnp.zeros((8, LANES), jnp.float32)
        for k in range(cap):
            acc = acc + jnp.where(spot == pairs[k], means[k : k + 1, :], 0.0)
        out[at] = acc

    def step(i, carry):
        for u in range(2):
            score(own, 2 * i + u, 2 * i + u)
            score(other, 2 * i + u, blocks + 2 * i + u)
        return carry

    lax.fori_loop(0, blocks // 2, step, 0)


def beam_kernel(own, other, doc, total):
    @pl.when(pl.program_id(0) == 0)
    def _():
        total[...] = jnp.zeros_like(total)

    left = jnp.concatenate([own[...], other[...]], axis=0)
    total[...] += lax.dot_general(left, doc[...], NT, preferred_element_type=jnp.float32)


def last_kernel(cfg, me_ref, own, other, doc, first, *refs):
    masks, parts, cand_at, blocks = cfg
    codes, scores, out, last = refs[:4], refs[4:6], refs[6], refs[7]
    stride = codes[0].shape[0] // blocks
    beam_kernel(own, other, doc, last)

    @pl.when(pl.program_id(0) == pl.num_programs(0) - 1)
    def _():
        me = me_ref[0]
        lane = ids((8, LANES), 1)
        nodes = last.shape[1]

        for m in masks[0]:
            for side in range(2):
                half, t = divmod(masks[0].index(m), blocks)
                table = codes[2 * half + side][(t + 1) * stride - 16 : (t + 1) * stride, :].astype(jnp.float32)[:8]
                low = pltpu.roll(table, LANES - cand_at, axis=1).astype(jnp.int32)
                table = table.astype(jnp.int32)
                owner, high = table // parts, table % parts
                slot = high * 256 + low
                within, page = slot % LANES, slot // LANES
                ats = [(side * 2 * blocks + masks[k].index(m)) * 8 for k in (1, 2)]
                rows = first[ats[0] : ats[0] + 8, :] + last[ats[1] : ats[1] + 8, :]
                found = jnp.zeros((8, LANES), jnp.float32)
                for g in range(nodes // LANES):
                    here = jnp.take_along_axis(rows[:, g * LANES : (g + 1) * LANES], within, axis=1)
                    found = jnp.where(page == g, here, found)
                found = jnp.where(owner == me, found, 0.0)
                out[me ^ (m + side)] = jnp.where(lane < cand_at, found, scores[half][side * blocks + t])


def sum_kernel(rounds, front, cands, parts, beam, maxsim):
    total = parts[0]
    for i in range(1, parts.shape[0]):
        total = total + parts[i]
    for r in range(rounds):
        beam[r] = (total if r == 0 else pltpu.roll(total, LANES - r * front, axis=1))[:, :front]
    maxsim[...] = pltpu.roll(total, LANES - rounds * front, axis=1)[:, :cands]


def local(n, query_fde, doc_fde, frontier_owner, frontier_slot, query_tokens, passage_tiles, passage_len, cand_owner, cand_slot):
    rounds, queries, front = frontier_owner.shape
    cands = cand_slot.shape[1]
    nodes, fde = doc_fde.shape
    qt, dim = query_tokens.shape[1:]
    parts = nodes // 256
    cand_at = rounds * front
    assert n & (n - 1) == 0 and queries == 8 and dim == LANES and nodes % 256 == 0
    assert cand_at + max(cand_at, cands) <= LANES and n * parts <= 256 and passage_tiles.shape[0] <= 256
    me = lax.axis_index("dom").astype(jnp.int32)
    stride = queries * qt + 16
    blocks = n // 4
    orders = orders_of(n)
    masks = [sources_of(o) for o in orders]

    pairs_count = queries * cands
    cap = max(2, min(pairs_count, 2 * pairs_count // n))
    slots = n * cap
    assert slots % LANES == 0 and slots <= 4 * LANES and LANES % cap == 0 and pairs_count <= 256
    packed = pl.pallas_call(
        functools.partial(prep_kernel, parts, slots, cap),
        out_shape=jax.ShapeDtypeStruct((stride, dim), jnp.bfloat16),
        in_specs=[VMEM] * 5,
        out_specs=VMEM,
        name="pack",
    )(frontier_owner, frontier_slot, cand_owner.reshape(queries, cands), cand_slot, query_tokens.reshape(queries * qt, dim))
    half = fde // 2
    starts = [packed, query_fde[:, :half], query_fde[:, half:]]
    stages = len(orders[0])

    @functools.cache
    def gathered(k, step):
        if step == 0:
            return starts[k]
        return jnp.concatenate([gathered(k, step - 1), arrived(k, step - 1)], axis=0)

    @functools.cache
    def arrived(k, step):
        mine = gathered(k, step)
        if (k, step) in TIES:
            mine = lax.optimization_barrier((mine, arrived(*TIES[k, step])))[0]
        return exchange(mine, orders[k][step], n)

    tok = [gathered(0, stages - 1), arrived(0, stages - 1)]
    tok = [(tok[0], exchange(tok[0], 1, n)), tok[1]]

    pt = passage_tiles.shape[1]
    score = lambda own, other: pl.pallas_call(
            functools.partial(maxsim_kernel, cand_at, cands, cap),
            out_shape=jax.ShapeDtypeStruct((n // 2, 8, LANES), jnp.float32),
            grid_spec=pltpu.PrefetchScalarGridSpec(
                num_scalar_prefetch=2,
                grid=(),
                in_specs=[VMEM] * 3,
                out_specs=VMEM,
                scratch_shapes=[
                    pltpu.VMEM((n // 2, LANES), jnp.int32),
                    pltpu.SMEM((n // 2, LANES), jnp.int32),
                    pltpu.SemaphoreType.DMA,
                ],
            ),
            compiler_params=pltpu.CompilerParams(vmem_limit_bytes=16 << 20),
            cost_estimate=pl.CostEstimate(flops=8 * slots * pt * qt * dim, bytes_accessed=8 << 20, transcendentals=0),
            name="maxsim",
        )(me.reshape(1), passage_len, own, other, passage_tiles)

    early = score(*tok[0])
    late, early = lax.optimization_barrier((tok[1], early))
    late_other = exchange(late, 1, n)
    a_own, b_own, late_other = lax.optimization_barrier((gathered(1, stages), gathered(2, stages), late_other))
    tok = [tok[0], (late, late_other)]
    maxsim = [early, score(*tok[1])]
    a_other, b_other = exchange(a_own, 1, n), exchange(b_own, 1, n)

    block = math.gcd(half, 1280)
    steps = half // block
    rows = n * 8
    full = lambda shape: pl.BlockSpec(shape, lambda i, *_: (0,) * len(shape))
    left = pl.BlockSpec((rows // 2, block), lambda i, *_: (0, i))
    doc = lambda first: pl.BlockSpec((nodes, block), lambda i, *_: (0, first + i))
    partial = jax.ShapeDtypeStruct((rows, nodes), jnp.float32)
    cost = pl.CostEstimate(flops=2 * rows * nodes * half, bytes_accessed=2 * (rows + nodes) * half, transcendentals=0)
    first = pl.pallas_call(
        beam_kernel,
        out_shape=partial,
        grid=(steps,),
        in_specs=[left, left, doc(0)],
        out_specs=full(partial.shape),
        compiler_params=pltpu.CompilerParams(vmem_limit_bytes=16 << 20),
        cost_estimate=cost,
        name="beam",
    )(a_own, a_other, doc_fde)
    codes = [*tok[0], *tok[1]]
    scored = pl.pallas_call(
        functools.partial(last_kernel, (masks, parts, cand_at, blocks)),
        out_shape=jax.ShapeDtypeStruct((n, 8, LANES), jnp.float32),
        grid_spec=pltpu.PrefetchScalarGridSpec(
            num_scalar_prefetch=1,
            grid=(steps,),
            in_specs=[left, left, doc(steps)] + [full(x.shape) for x in (first, *codes, *maxsim)],
            out_specs=full((n, 8, LANES)),
            scratch_shapes=[pltpu.VMEM(partial.shape, jnp.float32)],
        ),
        compiler_params=pltpu.CompilerParams(vmem_limit_bytes=24 << 20),
        cost_estimate=cost,
        name="beam_last",
    )(me.reshape(1), b_own, b_other, doc_fde, first, *codes, *maxsim)

    returned = lax.all_to_all(scored, "dom", split_axis=0, concat_axis=0, tiled=True)
    return pl.pallas_call(
        functools.partial(sum_kernel, rounds, front, cands),
        out_shape=(
            jax.ShapeDtypeStruct((rounds, queries, front), jnp.float32),
            jax.ShapeDtypeStruct((queries, cands), jnp.float32),
        ),
        in_specs=[VMEM],
        out_specs=(VMEM, VMEM),
        name="collect",
    )(returned)


def solution(mesh):
    in_specs = (
        P(("rep", "dom"), None),
        P("dom", None),
        P(None, ("rep", "dom"), None),
        P(None, ("rep", "dom"), None),
        P(("rep", "dom"), None, None),
        P("dom", None, None),
        P("dom"),
        P(("rep", "dom"), None, None),
        P(("rep", "dom"), None),
    )
    out_specs = (P(None, ("rep", "dom"), None), P(("rep", "dom"), None))
    return jax.shard_map(
        functools.partial(local, mesh.shape["dom"]), mesh=mesh, in_specs=in_specs, out_specs=out_specs, check_vma=False
    )
```

```python
import functools
import math

import jax
import jax.numpy as jnp
from jax import lax
from jax.experimental import pallas as pl
from jax.experimental.pallas import tpu as pltpu
from jax.sharding import PartitionSpec as P

masked_value = -1e30
LANES = 128
VMEM = pl.BlockSpec(memory_space=pltpu.VMEM)
NT = (((1,), (1,)), ((), ()))


def sources_of(order):
    masks = [0]
    for bit in order:
        masks = masks + [m ^ bit for m in masks]
    return masks


def orders_of(n):
    bits = [1 << i for i in range(1, n.bit_length() - 1)]
    far, rest = bits[-1:], bits[:-1]
    return [[16, 2, 4, 8], [16, 8, 2, 4], [16, 4, 8, 2]]


TIES = {}


def exchange(x, bit, n):
    return lax.ppermute(x, "dom", [(i, i ^ bit) for i in range(n)])


def place(values, offset):
    w = values.shape[1]
    where = lax.broadcasted_iota(jnp.int32, (w, LANES), 0) + offset
    lane = lax.broadcasted_iota(jnp.int32, (w, LANES), 1)
    return jnp.dot(
        values.astype(jnp.float32).astype(jnp.bfloat16),
        (where == lane).astype(jnp.float32).astype(jnp.bfloat16),
        preferred_element_type=jnp.float32,
    )


def ids(shape, axis):
    return lax.broadcasted_iota(jnp.int32, shape, axis)


def exact(values):
    return values.astype(jnp.float32).astype(jnp.bfloat16)


def pick(a, b):
    return jnp.dot(exact(a), exact(b), preferred_element_type=jnp.float32)


def prep_kernel(parts, slots, cap, fo, fs, co, cs, tok, out):
    rounds, queries, front = fo.shape
    rows, cands = tok.shape[0], co.shape[1]
    pairs = queries * cands
    low_at = rounds * front
    codes = jnp.zeros((queries, LANES), jnp.float32)
    for r in range(rounds):
        codes = codes + place(fo[r] * parts + (fs[r] >> 8), r * front)
        codes = codes + place(fs[r] & 255, low_at + r * front)

    across = (ids((cands, pairs), 1) % cands == ids((cands, pairs), 0))
    mine = ids((queries, pairs), 1) // cands == ids((queries, pairs), 0)
    line = lambda v: jnp.sum(jnp.where(mine, pick(v, across), 0.0), axis=0, keepdims=True)
    owner_line, slot_line = line(co[...]), line(cs[...])
    down = ids((pairs, queries), 0) // cands == ids((pairs, queries), 1)
    here = ids((pairs, cands), 0) % cands == ids((pairs, cands), 1)
    owner = jnp.sum(jnp.where(here, pick(down, co[...]), 0.0), axis=1, keepdims=True)
    earlier = (owner == owner_line) & (ids((pairs, pairs), 1) < ids((pairs, pairs), 0))
    position = jnp.sum(jnp.where(earlier, 1.0, 0.0), axis=1, keepdims=True)
    target = (owner * cap + position).astype(jnp.int32)
    number = (ids((1, pairs), 1) + 1).astype(jnp.float32)
    table = jnp.zeros((8, LANES), jnp.float32)
    for g in range(slots // LANES):
        row = ids((8, pairs), 0)
        values = jnp.where(row == 2 * g, number, jnp.where(row == 2 * g + 1, slot_line, 0.0))
        table = table + pick(values, target == ids((pairs, LANES), 1) + g * LANES)
    out[:rows, :] = tok[...]
    out[rows:, :] = jnp.concatenate([codes, table], axis=0).astype(jnp.bfloat16)


def maxsim_kernel(cand_at, cands, cap, me_ref, lens, own, other, tiles, out, listed, lst, sem):
    blocks = out.shape[0] // 2
    stride = own.shape[0] // blocks
    pt = tiles.shape[1]
    qt = (stride - 16) // 8
    start = me_ref[0] * cap
    row, lane = ids((8, LANES), 0), ids((8, LANES), 1)
    group = start // LANES
    for side, ref in enumerate((own, other)):
        for b in range(blocks):
            table = ref[(b + 1) * stride - 16 : (b + 1) * stride, :].astype(jnp.float32)[8:]
            weight = jnp.where(row == 2 * group, 256.0, jnp.where(row == 2 * group + 1, 1.0, 0.0))
            at = side * blocks + b
            listed[at : at + 1, :] = jnp.sum(table * weight, axis=0, keepdims=True).astype(jnp.int32)
    listed[...] = pltpu.roll(listed[...], lax.rem(LANES - start % LANES, LANES), axis=1)
    copy = pltpu.make_async_copy(listed, lst, sem)
    copy.start()
    copy.wait()

    spot = jnp.where((lane >= cand_at) & (lane < cand_at + cands), row * cands + lane - cand_at, -1)
    token = ids((pt, 2 * qt), 0)
    right = ids((1, 2 * qt), 1) >= qt
    empty = jnp.zeros((qt, LANES), own.dtype)

    def score(ref, b, at):
        tops, pairs = [], []
        for k in range(0, cap, 2):
            slots, tokens = [], []
            for entry in (lst[at, k], lst[at, k + 1]):
                pair = (entry >> 8) - 1
                query = jnp.maximum(pair, 0) // cands
                slots.append(entry & 255)
                tokens.append(ref[pl.ds(pl.multiple_of(b * stride + query * qt, 16), qt), :])
                pairs.append(jnp.where(pair < 0, -2, pair))
            data = jnp.concatenate([tiles[slots[0]], tiles[slots[1]]], axis=1)
            weights = jnp.concatenate(
                [jnp.concatenate([tokens[0], empty], axis=1), jnp.concatenate([empty, tokens[1]], axis=1)], axis=0
            )
            sim = lax.dot_general(data, weights, NT, preferred_element_type=jnp.float32)
            length = jnp.where(right, lens[slots[1]], lens[slots[0]])
            sim = jnp.where(token < length, sim, masked_value)
            tops.append(jnp.max(sim, axis=0, keepdims=True))
        tops = jnp.concatenate(tops, axis=0)
        first = jnp.sum(jnp.where(right, 0.0, tops), axis=1, keepdims=True) * (1.0 / qt)
        second = jnp.sum(jnp.where(right, tops, 0.0), axis=1, keepdims=True) * (1.0 / qt)
        acc = jnp.zeros((8, LANES), jnp.float32)
        for k in range(cap):
            means = second if k % 2 else first
            acc = acc + jnp.where(spot == pairs[k], means[k // 2 : k // 2 + 1, :], 0.0)
        out[at] = acc

    def step(i, carry):
        for u in range(4):
            score(own, 4 * i + u, 4 * i + u)
            score(other, 4 * i + u, blocks + 4 * i + u)
        return carry

    lax.fori_loop(0, blocks // 4, step, 0)


def beam_kernel(own, other, doc, total):
    @pl.when(pl.program_id(0) == 0)
    def _():
        total[...] = jnp.zeros_like(total)

    left = jnp.concatenate([own[...], other[...]], axis=0)
    total[...] += lax.dot_general(left, doc[...], NT, preferred_element_type=jnp.float32)


def last_kernel(cfg, me_ref, own, other, doc, first, *refs):
    masks, parts, cand_at, blocks = cfg
    codes, scores, out, last = refs[:4], refs[4:6], refs[6], refs[7]
    stride = codes[0].shape[0] // blocks
    beam_kernel(own, other, doc, last)

    @pl.when(pl.program_id(0) == pl.num_programs(0) - 1)
    def _():
        me = me_ref[0]
        lane = ids((8, LANES), 1)
        nodes = last.shape[1]

        for m in masks[0]:
            for side in range(2):
                half, t = divmod(masks[0].index(m), blocks)
                table = codes[2 * half + side][(t + 1) * stride - 16 : (t + 1) * stride, :].astype(jnp.float32)[:8]
                low = pltpu.roll(table, LANES - cand_at, axis=1).astype(jnp.int32)
                table = table.astype(jnp.int32)
                owner, high = table // parts, table % parts
                slot = high * 256 + low
                within, page = slot % LANES, slot // LANES
                ats = [(side * 2 * blocks + masks[k].index(m)) * 8 for k in (1, 2)]
                rows = first[ats[0] : ats[0] + 8, :] + last[ats[1] : ats[1] + 8, :]
                found = jnp.zeros((8, LANES), jnp.float32)
                for g in range(nodes // LANES):
                    here = jnp.take_along_axis(rows[:, g * LANES : (g + 1) * LANES], within, axis=1)
                    found = jnp.where(page == g, here, found)
                found = jnp.where(owner == me, found, 0.0)
                out[me ^ (m + side)] = jnp.where(lane < cand_at, found, scores[half][side * blocks + t])


def sum_kernel(rounds, front, cands, parts, beam, maxsim):
    total = parts[0]
    for i in range(1, parts.shape[0]):
        total = total + parts[i]
    for r in range(rounds):
        beam[r] = (total if r == 0 else pltpu.roll(total, LANES - r * front, axis=1))[:, :front]
    maxsim[...] = pltpu.roll(total, LANES - rounds * front, axis=1)[:, :cands]


def local(n, query_fde, doc_fde, frontier_owner, frontier_slot, query_tokens, passage_tiles, passage_len, cand_owner, cand_slot):
    rounds, queries, front = frontier_owner.shape
    cands = cand_slot.shape[1]
    nodes, fde = doc_fde.shape
    qt, dim = query_tokens.shape[1:]
    parts = nodes // 256
    cand_at = rounds * front
    assert n & (n - 1) == 0 and queries == 8 and dim == LANES and nodes % 256 == 0
    assert cand_at + max(cand_at, cands) <= LANES and n * parts <= 256 and passage_tiles.shape[0] <= 256
    me = lax.axis_index("dom").astype(jnp.int32)
    stride = queries * qt + 16
    blocks = n // 4
    orders = orders_of(n)
    masks = [sources_of(o) for o in orders]

    pairs_count = queries * cands
    cap = max(2, min(pairs_count, 2 * pairs_count // n))
    slots = n * cap
    assert slots % LANES == 0 and slots <= 4 * LANES and LANES % cap == 0 and pairs_count <= 256
    packed = pl.pallas_call(
        functools.partial(prep_kernel, parts, slots, cap),
        out_shape=jax.ShapeDtypeStruct((stride, dim), jnp.bfloat16),
        in_specs=[VMEM] * 5,
        out_specs=VMEM,
        name="pack",
    )(frontier_owner, frontier_slot, cand_owner.reshape(queries, cands), cand_slot, query_tokens.reshape(queries * qt, dim))
    half = fde // 2
    starts = [packed, query_fde[:, :half], query_fde[:, half:]]
    stages = len(orders[0])

    @functools.cache
    def gathered(k, step):
        if step == 0:
            return starts[k]
        return jnp.concatenate([gathered(k, step - 1), arrived(k, step - 1)], axis=0)

    @functools.cache
    def arrived(k, step):
        mine = gathered(k, step)
        if (k, step) in TIES:
            mine = lax.optimization_barrier((mine, arrived(*TIES[k, step])))[0]
        return exchange(mine, orders[k][step], n)

    tok = [gathered(0, stages - 1), arrived(0, stages - 1)]
    tok = [(tok[0], exchange(tok[0], 1, n)), tok[1]]

    pt = passage_tiles.shape[1]
    score = lambda own, other: pl.pallas_call(
            functools.partial(maxsim_kernel, cand_at, cands, cap),
            out_shape=jax.ShapeDtypeStruct((n // 2, 8, LANES), jnp.float32),
            grid_spec=pltpu.PrefetchScalarGridSpec(
                num_scalar_prefetch=2,
                grid=(),
                in_specs=[VMEM] * 3,
                out_specs=VMEM,
                scratch_shapes=[
                    pltpu.VMEM((n // 2, LANES), jnp.int32),
                    pltpu.SMEM((n // 2, LANES), jnp.int32),
                    pltpu.SemaphoreType.DMA,
                ],
            ),
            compiler_params=pltpu.CompilerParams(vmem_limit_bytes=16 << 20),
            cost_estimate=pl.CostEstimate(flops=8 * slots * pt * qt * dim, bytes_accessed=8 << 20, transcendentals=0),
            name="maxsim",
        )(me.reshape(1), passage_len, own, other, passage_tiles)

    early = score(*tok[0])
    late, early = lax.optimization_barrier((tok[1], early))
    late_other = exchange(late, 1, n)
    a_own, b_own, late_other = lax.optimization_barrier((gathered(1, stages), gathered(2, stages), late_other))
    tok = [tok[0], (late, late_other)]
    maxsim = [early, score(*tok[1])]
    a_other, b_other = exchange(a_own, 1, n), exchange(b_own, 1, n)

    block = half
    steps = half // block
    rows = n * 8
    full = lambda shape: pl.BlockSpec(shape, lambda i, *_: (0,) * len(shape))
    left = pl.BlockSpec((rows // 2, block), lambda i, *_: (0, i))
    doc = lambda first: pl.BlockSpec((nodes, block), lambda i, *_: (0, first + i))
    partial = jax.ShapeDtypeStruct((rows, nodes), jnp.float32)
    cost = pl.CostEstimate(flops=2 * rows * nodes * half, bytes_accessed=2 * (rows + nodes) * half, transcendentals=0)
    first = pl.pallas_call(
        beam_kernel,
        out_shape=partial,
        grid=(steps,),
        in_specs=[left, left, doc(0)],
        out_specs=full(partial.shape),
        compiler_params=pltpu.CompilerParams(vmem_limit_bytes=16 << 20),
        cost_estimate=cost,
        name="beam",
    )(a_own, a_other, doc_fde)
    codes = [*tok[0], *tok[1]]
    scored = pl.pallas_call(
        functools.partial(last_kernel, (masks, parts, cand_at, blocks)),
        out_shape=jax.ShapeDtypeStruct((n, 8, LANES), jnp.float32),
        grid_spec=pltpu.PrefetchScalarGridSpec(
            num_scalar_prefetch=1,
            grid=(steps,),
            in_specs=[left, left, doc(steps)] + [full(x.shape) for x in (first, *codes, *maxsim)],
            out_specs=full((n, 8, LANES)),
            scratch_shapes=[pltpu.VMEM(partial.shape, jnp.float32)],
        ),
        compiler_params=pltpu.CompilerParams(vmem_limit_bytes=24 << 20),
        cost_estimate=cost,
        name="beam_last",
    )(me.reshape(1), b_own, b_other, doc_fde, first, *codes, *maxsim)

    returned = lax.all_to_all(scored, "dom", split_axis=0, concat_axis=0, tiled=True)
    return pl.pallas_call(
        functools.partial(sum_kernel, rounds, front, cands),
        out_shape=(
            jax.ShapeDtypeStruct((rounds, queries, front), jnp.float32),
            jax.ShapeDtypeStruct((queries, cands), jnp.float32),
        ),
        in_specs=[VMEM],
        out_specs=(VMEM, VMEM),
        name="collect",
    )(returned)


def solution(mesh):
    in_specs = (
        P(("rep", "dom"), None),
        P("dom", None),
        P(None, ("rep", "dom"), None),
        P(None, ("rep", "dom"), None),
        P(("rep", "dom"), None, None),
        P("dom", None, None),
        P("dom"),
        P(("rep", "dom"), None, None),
        P(("rep", "dom"), None),
    )
    out_specs = (P(None, ("rep", "dom"), None), P(("rep", "dom"), None))
    return jax.shard_map(
        functools.partial(local, mesh.shape["dom"]), mesh=mesh, in_specs=in_specs, out_specs=out_specs, check_vma=False
    )
```

```python
import functools
import math

import jax
import jax.numpy as jnp
from jax import lax
from jax.experimental import pallas as pl
from jax.experimental.pallas import tpu as pltpu
from jax.sharding import PartitionSpec as P

masked_value = -1e30
LANES = 128
VMEM = pl.BlockSpec(memory_space=pltpu.VMEM)
NT = (((1,), (1,)), ((), ()))


def sources_of(order):
    masks = [0]
    for bit in order:
        masks = masks + [m ^ bit for m in masks]
    return masks


def orders_of(n):
    bits = [1 << i for i in range(1, n.bit_length() - 1)]
    far, rest = bits[-1:], bits[:-1]
    return [[16, 2, 4, 8], [16, 8, 2, 4], [16, 4, 8, 2]]


TIES = {}


def exchange(x, bit, n):
    return lax.ppermute(x, "dom", [(i, i ^ bit) for i in range(n)])


def place(values, offset):
    w = values.shape[1]
    where = lax.broadcasted_iota(jnp.int32, (w, LANES), 0) + offset
    lane = lax.broadcasted_iota(jnp.int32, (w, LANES), 1)
    return jnp.dot(
        values.astype(jnp.float32).astype(jnp.bfloat16),
        (where == lane).astype(jnp.float32).astype(jnp.bfloat16),
        preferred_element_type=jnp.float32,
    )


def ids(shape, axis):
    return lax.broadcasted_iota(jnp.int32, shape, axis)


def exact(values):
    return values.astype(jnp.float32).astype(jnp.bfloat16)


def pick(a, b):
    return jnp.dot(exact(a), exact(b), preferred_element_type=jnp.float32)


def prep_kernel(parts, slots, cap, fo, fs, co, cs, tok, out):
    rounds, queries, front = fo.shape
    rows, cands = tok.shape[0], co.shape[1]
    pairs = queries * cands
    low_at = rounds * front
    codes = jnp.zeros((queries, LANES), jnp.float32)
    for r in range(rounds):
        codes = codes + place(fo[r] * parts + (fs[r] >> 8), r * front)
        codes = codes + place(fs[r] & 255, low_at + r * front)

    across = (ids((cands, pairs), 1) % cands == ids((cands, pairs), 0))
    mine = ids((queries, pairs), 1) // cands == ids((queries, pairs), 0)
    line = lambda v: jnp.sum(jnp.where(mine, pick(v, across), 0.0), axis=0, keepdims=True)
    owner_line, slot_line = line(co[...]), line(cs[...])
    down = ids((pairs, queries), 0) // cands == ids((pairs, queries), 1)
    here = ids((pairs, cands), 0) % cands == ids((pairs, cands), 1)
    owner = jnp.sum(jnp.where(here, pick(down, co[...]), 0.0), axis=1, keepdims=True)
    earlier = (owner == owner_line) & (ids((pairs, pairs), 1) < ids((pairs, pairs), 0))
    position = jnp.sum(jnp.where(earlier, 1.0, 0.0), axis=1, keepdims=True)
    target = (owner * cap + position).astype(jnp.int32)
    number = (ids((1, pairs), 1) + 1).astype(jnp.float32)
    table = jnp.zeros((8, LANES), jnp.float32)
    for g in range(slots // LANES):
        row = ids((8, pairs), 0)
        values = jnp.where(row == 2 * g, number, jnp.where(row == 2 * g + 1, slot_line, 0.0))
        table = table + pick(values, target == ids((pairs, LANES), 1) + g * LANES)
    out[:rows, :] = tok[...]
    out[rows:, :] = jnp.concatenate([codes, table], axis=0).astype(jnp.bfloat16)


def maxsim_kernel(cand_at, cands, cap, me_ref, lens, *refs):
    *sides, tiles, out, listed, lst, sem = refs
    blocks = out.shape[0] // len(sides)
    stride = sides[0].shape[0] // blocks
    pt = tiles.shape[1]
    qt = (stride - 16) // 8
    start = me_ref[0] * cap
    row, lane = ids((8, LANES), 0), ids((8, LANES), 1)
    group = start // LANES
    for side, ref in enumerate(sides):
        for b in range(blocks):
            table = ref[(b + 1) * stride - 16 : (b + 1) * stride, :].astype(jnp.float32)[8:]
            weight = jnp.where(row == 2 * group, 256.0, jnp.where(row == 2 * group + 1, 1.0, 0.0))
            at = side * blocks + b
            listed[at : at + 1, :] = jnp.sum(table * weight, axis=0, keepdims=True).astype(jnp.int32)
    listed[...] = pltpu.roll(listed[...], lax.rem(LANES - start % LANES, LANES), axis=1)
    copy = pltpu.make_async_copy(listed, lst, sem)
    copy.start()
    copy.wait()

    spot = jnp.where((lane >= cand_at) & (lane < cand_at + cands), row * cands + lane - cand_at, -1)
    token = ids((pt, 2 * qt), 0)
    right = ids((1, 2 * qt), 1) >= qt
    empty = jnp.zeros((qt, LANES), sides[0].dtype)

    def score(ref, b, at):
        tops, pairs = [], []
        for k in range(0, cap, 2):
            slots, tokens = [], []
            for entry in (lst[at, k], lst[at, k + 1]):
                pair = (entry >> 8) - 1
                query = jnp.maximum(pair, 0) // cands
                slots.append(entry & 255)
                tokens.append(ref[pl.ds(pl.multiple_of(b * stride + query * qt, 16), qt), :])
                pairs.append(jnp.where(pair < 0, -2, pair))
            data = jnp.concatenate([tiles[slots[0]], tiles[slots[1]]], axis=1)
            weights = jnp.concatenate(
                [jnp.concatenate([tokens[0], empty], axis=1), jnp.concatenate([empty, tokens[1]], axis=1)], axis=0
            )
            sim = lax.dot_general(data, weights, NT, preferred_element_type=jnp.float32)
            length = jnp.where(right, lens[slots[1]], lens[slots[0]])
            sim = jnp.where(token < length, sim, masked_value)
            tops.append(jnp.max(sim, axis=0, keepdims=True))
        tops = jnp.concatenate(tops, axis=0)
        first = jnp.sum(jnp.where(right, 0.0, tops), axis=1, keepdims=True) * (1.0 / qt)
        second = jnp.sum(jnp.where(right, tops, 0.0), axis=1, keepdims=True) * (1.0 / qt)
        acc = jnp.zeros((8, LANES), jnp.float32)
        for k in range(cap):
            means = second if k % 2 else first
            acc = acc + jnp.where(spot == pairs[k], means[k // 2 : k // 2 + 1, :], 0.0)
        out[at] = acc

    together = 8 // len(sides)

    def step(i, carry):
        for u in range(together):
            for side, ref in enumerate(sides):
                score(ref, together * i + u, side * blocks + together * i + u)
        return carry

    lax.fori_loop(0, blocks // together, step, 0)


def beam_kernel(own, other, doc, total):
    @pl.when(pl.program_id(0) == 0)
    def _():
        total[...] = jnp.zeros_like(total)

    left = jnp.concatenate([own[...], other[...]], axis=0)
    total[...] += lax.dot_general(left, doc[...], NT, preferred_element_type=jnp.float32)


def last_kernel(cfg, me_ref, own, other, doc, first, *refs):
    masks, parts, cand_at, blocks = cfg
    codes, scores, out, last = refs[:4], refs[4:7], refs[7], refs[8]
    stride = codes[0].shape[0] // blocks
    beam_kernel(own, other, doc, last)

    @pl.when(pl.program_id(0) == pl.num_programs(0) - 1)
    def _():
        me = me_ref[0]
        lane = ids((8, LANES), 1)
        nodes = last.shape[1]

        for m in masks[0]:
            for side in range(2):
                half, t = divmod(masks[0].index(m), blocks)
                table = codes[2 * half + side][(t + 1) * stride - 16 : (t + 1) * stride, :].astype(jnp.float32)[:8]
                low = pltpu.roll(table, LANES - cand_at, axis=1).astype(jnp.int32)
                table = table.astype(jnp.int32)
                owner, high = table // parts, table % parts
                slot = high * 256 + low
                within, page = slot % LANES, slot // LANES
                ats = [(side * 2 * blocks + masks[k].index(m)) * 8 for k in (1, 2)]
                rows = first[ats[0] : ats[0] + 8, :] + last[ats[1] : ats[1] + 8, :]
                found = jnp.zeros((8, LANES), jnp.float32)
                for g in range(nodes // LANES):
                    here = jnp.take_along_axis(rows[:, g * LANES : (g + 1) * LANES], within, axis=1)
                    found = jnp.where(page == g, here, found)
                found = jnp.where(owner == me, found, 0.0)
                out[me ^ (m + side)] = jnp.where(lane < cand_at, found, (scores[0][side * blocks + t] if half == 0 else scores[1 + side][t]))


def sum_kernel(rounds, front, cands, parts, beam, maxsim):
    total = parts[0]
    for i in range(1, parts.shape[0]):
        total = total + parts[i]
    for r in range(rounds):
        beam[r] = (total if r == 0 else pltpu.roll(total, LANES - r * front, axis=1))[:, :front]
    maxsim[...] = pltpu.roll(total, LANES - rounds * front, axis=1)[:, :cands]


def local(n, query_fde, doc_fde, frontier_owner, frontier_slot, query_tokens, passage_tiles, passage_len, cand_owner, cand_slot):
    rounds, queries, front = frontier_owner.shape
    cands = cand_slot.shape[1]
    nodes, fde = doc_fde.shape
    qt, dim = query_tokens.shape[1:]
    parts = nodes // 256
    cand_at = rounds * front
    assert n & (n - 1) == 0 and queries == 8 and dim == LANES and nodes % 256 == 0
    assert cand_at + max(cand_at, cands) <= LANES and n * parts <= 256 and passage_tiles.shape[0] <= 256
    me = lax.axis_index("dom").astype(jnp.int32)
    stride = queries * qt + 16
    blocks = n // 4
    orders = orders_of(n)
    masks = [sources_of(o) for o in orders]

    pairs_count = queries * cands
    cap = max(2, min(pairs_count, 2 * pairs_count // n))
    slots = n * cap
    assert slots % LANES == 0 and slots <= 4 * LANES and LANES % cap == 0 and pairs_count <= 256
    half = fde // 2
    query_tokens, left_part, right_part = lax.optimization_barrier(
        (query_tokens, query_fde[:, :half], query_fde[:, half:])
    )
    packed = pl.pallas_call(
        functools.partial(prep_kernel, parts, slots, cap),
        out_shape=jax.ShapeDtypeStruct((stride, dim), jnp.bfloat16),
        in_specs=[VMEM] * 5,
        out_specs=VMEM,
        name="pack",
    )(frontier_owner, frontier_slot, cand_owner.reshape(queries, cands), cand_slot, query_tokens.reshape(queries * qt, dim))
    starts = [packed, left_part, right_part]
    stages = len(orders[0])

    @functools.cache
    def gathered(k, step):
        if step == 0:
            return starts[k]
        return jnp.concatenate([gathered(k, step - 1), arrived(k, step - 1)], axis=0)

    @functools.cache
    def arrived(k, step):
        mine = gathered(k, step)
        if (k, step) in TIES:
            mine = lax.optimization_barrier((mine, arrived(*TIES[k, step])))[0]
        return exchange(mine, orders[k][step], n)

    tok = [gathered(0, stages - 1), arrived(0, stages - 1)]
    tok = [(tok[0], exchange(tok[0], 1, n)), tok[1]]

    pt = passage_tiles.shape[1]
    score = lambda *sides: pl.pallas_call(
            functools.partial(maxsim_kernel, cand_at, cands, cap),
            out_shape=jax.ShapeDtypeStruct((n // 4 * len(sides), 8, LANES), jnp.float32),
            grid_spec=pltpu.PrefetchScalarGridSpec(
                num_scalar_prefetch=2,
                grid=(),
                in_specs=[VMEM] * (len(sides) + 1),
                out_specs=VMEM,
                scratch_shapes=[
                    pltpu.VMEM((n // 4 * len(sides), LANES), jnp.int32),
                    pltpu.SMEM((n // 4 * len(sides), LANES), jnp.int32),
                    pltpu.SemaphoreType.DMA,
                ],
            ),
            compiler_params=pltpu.CompilerParams(vmem_limit_bytes=16 << 20),
            cost_estimate=pl.CostEstimate(flops=4 * len(sides) * slots * pt * qt * dim, bytes_accessed=8 << 20, transcendentals=0),
            name="maxsim",
        )(me.reshape(1), passage_len, *sides, passage_tiles)

    early = score(*tok[0])
    late, early = lax.optimization_barrier((tok[1], early))
    late_other = exchange(late, 1, n)
    maxsim = [early, score(late)]
    a_own, b_own, late_other, _ = lax.optimization_barrier((gathered(1, stages), gathered(2, stages), late_other, maxsim[1]))
    tok = [tok[0], (late, late_other)]
    maxsim.append(score(late_other))
    a_other, b_other = exchange(a_own, 1, n), exchange(b_own, 1, n)

    block = half
    steps = half // block
    rows = n * 8
    full = lambda shape: pl.BlockSpec(shape, lambda i, *_: (0,) * len(shape))
    left = pl.BlockSpec((rows // 2, block), lambda i, *_: (0, i))
    doc = lambda first: pl.BlockSpec((nodes, block), lambda i, *_: (0, first + i))
    partial = jax.ShapeDtypeStruct((rows, nodes), jnp.float32)
    cost = pl.CostEstimate(flops=2 * rows * nodes * half, bytes_accessed=2 * (rows + nodes) * half, transcendentals=0)
    first = pl.pallas_call(
        beam_kernel,
        out_shape=partial,
        grid=(steps,),
        in_specs=[left, left, doc(0)],
        out_specs=full(partial.shape),
        compiler_params=pltpu.CompilerParams(vmem_limit_bytes=16 << 20),
        cost_estimate=cost,
        name="beam",
    )(a_own, a_other, doc_fde)
    codes = [*tok[0], *tok[1]]
    scored = pl.pallas_call(
        functools.partial(last_kernel, (masks, parts, cand_at, blocks)),
        out_shape=jax.ShapeDtypeStruct((n, 8, LANES), jnp.float32),
        grid_spec=pltpu.PrefetchScalarGridSpec(
            num_scalar_prefetch=1,
            grid=(steps,),
            in_specs=[left, left, doc(steps)] + [full(x.shape) for x in (first, *codes, *maxsim)],
            out_specs=full((n, 8, LANES)),
            scratch_shapes=[pltpu.VMEM(partial.shape, jnp.float32)],
        ),
        compiler_params=pltpu.CompilerParams(vmem_limit_bytes=24 << 20),
        cost_estimate=cost,
        name="beam_last",
    )(me.reshape(1), b_own, b_other, doc_fde, first, *codes, *maxsim)

    returned = lax.all_to_all(scored, "dom", split_axis=0, concat_axis=0, tiled=True)
    return pl.pallas_call(
        functools.partial(sum_kernel, rounds, front, cands),
        out_shape=(
            jax.ShapeDtypeStruct((rounds, queries, front), jnp.float32),
            jax.ShapeDtypeStruct((queries, cands), jnp.float32),
        ),
        in_specs=[VMEM],
        out_specs=(VMEM, VMEM),
        name="collect",
    )(returned)


def solution(mesh):
    in_specs = (
        P(("rep", "dom"), None),
        P("dom", None),
        P(None, ("rep", "dom"), None),
        P(None, ("rep", "dom"), None),
        P(("rep", "dom"), None, None),
        P("dom", None, None),
        P("dom"),
        P(("rep", "dom"), None, None),
        P(("rep", "dom"), None),
    )
    out_specs = (P(None, ("rep", "dom"), None), P(("rep", "dom"), None))
    return jax.shard_map(
        functools.partial(local, mesh.shape["dom"]), mesh=mesh, in_specs=in_specs, out_specs=out_specs, check_vma=False
    )
```

```python
import functools
import math

import jax
import jax.numpy as jnp
from jax import lax
from jax.experimental import pallas as pl
from jax.experimental.pallas import tpu as pltpu
from jax.sharding import PartitionSpec as P

masked_value = -1e30
LANES = 128
VMEM = pl.BlockSpec(memory_space=pltpu.VMEM)
NT = (((1,), (1,)), ((), ()))


def sources_of(order):
    masks = [0]
    for bit in order:
        masks = masks + [m ^ bit for m in masks]
    return masks


def orders_of(n):
    bits = [1 << i for i in range(1, n.bit_length() - 1)]
    far, rest = bits[-1:], bits[:-1]
    return [[16, 2, 4, 8], [16, 8, 2, 4], [16, 4, 8, 2]]


def exchange(x, bit, n):
    return lax.ppermute(x, "dom", [(i, i ^ bit) for i in range(n)])


def place(values, offset):
    w = values.shape[1]
    where = lax.broadcasted_iota(jnp.int32, (w, LANES), 0) + offset
    lane = lax.broadcasted_iota(jnp.int32, (w, LANES), 1)
    return jnp.dot(
        values.astype(jnp.float32).astype(jnp.bfloat16),
        (where == lane).astype(jnp.float32).astype(jnp.bfloat16),
        preferred_element_type=jnp.float32,
    )


def ids(shape, axis):
    return lax.broadcasted_iota(jnp.int32, shape, axis)


def exact(values):
    return values.astype(jnp.float32).astype(jnp.bfloat16)


def pick(a, b):
    return jnp.dot(exact(a), exact(b), preferred_element_type=jnp.float32)


def prep_kernel(parts, slots, cap, fo, fs, co, cs, tok, out):
    rounds, queries, front = fo.shape
    rows, cands = tok.shape[0], co.shape[1]
    pairs = queries * cands
    low_at = rounds * front
    codes = jnp.zeros((queries, LANES), jnp.float32)
    for r in range(rounds):
        codes = codes + place(fo[r] * parts + (fs[r] >> 8), r * front)
        codes = codes + place(fs[r] & 255, low_at + r * front)

    across = (ids((cands, pairs), 1) % cands == ids((cands, pairs), 0))
    mine = ids((queries, pairs), 1) // cands == ids((queries, pairs), 0)
    line = lambda v: jnp.sum(jnp.where(mine, pick(v, across), 0.0), axis=0, keepdims=True)
    owner_line, slot_line = line(co[...]), line(cs[...])
    down = ids((pairs, queries), 0) // cands == ids((pairs, queries), 1)
    here = ids((pairs, cands), 0) % cands == ids((pairs, cands), 1)
    owner = jnp.sum(jnp.where(here, pick(down, co[...]), 0.0), axis=1, keepdims=True)
    earlier = (owner == owner_line) & (ids((pairs, pairs), 1) < ids((pairs, pairs), 0))
    position = jnp.sum(jnp.where(earlier, 1.0, 0.0), axis=1, keepdims=True)
    target = (owner * cap + position).astype(jnp.int32)
    number = (ids((1, pairs), 1) + 1).astype(jnp.float32)
    table = jnp.zeros((8, LANES), jnp.float32)
    for g in range(slots // LANES):
        row = ids((8, pairs), 0)
        values = jnp.where(row == 2 * g, number, jnp.where(row == 2 * g + 1, slot_line, 0.0))
        table = table + pick(values, target == ids((pairs, LANES), 1) + g * LANES)
    out[:rows, :] = tok[...]
    out[rows:, :] = jnp.concatenate([codes, table], axis=0).astype(jnp.bfloat16)


def maxsim_kernel(cand_at, cands, cap, me_ref, lens, *refs):
    *sides, tiles, out, listed, lst, sem = refs
    blocks = out.shape[0] // len(sides)
    stride = sides[0].shape[0] // blocks
    pt = tiles.shape[1]
    qt = (stride - 16) // 8
    start = me_ref[0] * cap
    row, lane = ids((8, LANES), 0), ids((8, LANES), 1)
    group = start // LANES
    for side, ref in enumerate(sides):
        for b in range(blocks):
            table = ref[(b + 1) * stride - 16 : (b + 1) * stride, :].astype(jnp.float32)[8:]
            weight = jnp.where(row == 2 * group, 256.0, jnp.where(row == 2 * group + 1, 1.0, 0.0))
            at = side * blocks + b
            listed[at : at + 1, :] = jnp.sum(table * weight, axis=0, keepdims=True).astype(jnp.int32)
    listed[...] = pltpu.roll(listed[...], lax.rem(LANES - start % LANES, LANES), axis=1)
    copy = pltpu.make_async_copy(listed, lst, sem)
    copy.start()
    copy.wait()

    spot = jnp.where((lane >= cand_at) & (lane < cand_at + cands), row * cands + lane - cand_at, -1)
    token = ids((pt, 2 * qt), 0)
    right = ids((1, 2 * qt), 1) >= qt
    empty = jnp.zeros((qt, LANES), sides[0].dtype)

    def score(ref, b, at):
        tops, pairs = [], []
        for k in range(0, cap, 2):
            slots, tokens = [], []
            for entry in (lst[at, k], lst[at, k + 1]):
                pair = (entry >> 8) - 1
                query = jnp.maximum(pair, 0) // cands
                slots.append(entry & 255)
                tokens.append(ref[pl.ds(pl.multiple_of(b * stride + query * qt, 16), qt), :])
                pairs.append(jnp.where(pair < 0, -2, pair))
            data = jnp.concatenate([tiles[slots[0]], tiles[slots[1]]], axis=1)
            weights = jnp.concatenate(
                [jnp.concatenate([tokens[0], empty], axis=1), jnp.concatenate([empty, tokens[1]], axis=1)], axis=0
            )
            sim = lax.dot_general(data, weights, NT, preferred_element_type=jnp.float32)
            length = jnp.where(right, lens[slots[1]], lens[slots[0]])
            sim = jnp.where(token < length, sim, masked_value)
            tops.append(jnp.max(sim, axis=0, keepdims=True))
        tops = jnp.concatenate(tops, axis=0)
        first = jnp.sum(jnp.where(right, 0.0, tops), axis=1, keepdims=True) * (1.0 / qt)
        second = jnp.sum(jnp.where(right, tops, 0.0), axis=1, keepdims=True) * (1.0 / qt)
        acc = jnp.zeros((8, LANES), jnp.float32)
        for k in range(cap):
            means = second if k % 2 else first
            acc = acc + jnp.where(spot == pairs[k], means[k // 2 : k // 2 + 1, :], 0.0)
        out[at] = acc

    together = 8 // len(sides)

    def step(i, carry):
        for u in range(together):
            for side, ref in enumerate(sides):
                score(ref, together * i + u, side * blocks + together * i + u)
        return carry

    lax.fori_loop(0, blocks // together, step, 0)


def beam_kernel(own, other, doc, total):
    left = jnp.concatenate([own[...], other[...]], axis=0)
    total[...] = lax.dot_general(left, doc[...], NT, preferred_element_type=jnp.float32)


def last_kernel(cfg, me_ref, own, other, doc, first, *refs):
    masks, parts, cand_at, blocks = cfg
    codes, scores, out, last = refs[:4], refs[4:7], refs[7], refs[8]
    stride = codes[0].shape[0] // blocks
    beam_kernel(own, other, doc, last)

    me = me_ref[0]
    lane = ids((8, LANES), 1)
    nodes = last.shape[1]

    for m in masks[0]:
        for side in range(2):
            half, t = divmod(masks[0].index(m), blocks)
            table = codes[2 * half + side][(t + 1) * stride - 16 : (t + 1) * stride, :].astype(jnp.float32)[:8]
            low = pltpu.roll(table, LANES - cand_at, axis=1).astype(jnp.int32)
            table = table.astype(jnp.int32)
            owner, high = table // parts, table % parts
            slot = high * 256 + low
            within, page = slot % LANES, slot // LANES
            ats = [(side * 2 * blocks + masks[k].index(m)) * 8 for k in (1, 2)]
            rows = first[ats[0] : ats[0] + 8, :] + last[ats[1] : ats[1] + 8, :]
            found = jnp.zeros((8, LANES), jnp.float32)
            for g in range(nodes // LANES):
                here = jnp.take_along_axis(rows[:, g * LANES : (g + 1) * LANES], within, axis=1)
                found = jnp.where(page == g, here, found)
            found = jnp.where(owner == me, found, 0.0)
            out[me ^ (m + side)] = jnp.where(lane < cand_at, found, (scores[0][side * blocks + t] if half == 0 else scores[1 + side][t]))


def local(n, query_fde, doc_fde, frontier_owner, frontier_slot, query_tokens, passage_tiles, passage_len, cand_owner, cand_slot):
    rounds, queries, front = frontier_owner.shape
    cands = cand_slot.shape[1]
    nodes, fde = doc_fde.shape
    qt, dim = query_tokens.shape[1:]
    parts = nodes // 256
    cand_at = rounds * front
    assert n & (n - 1) == 0 and queries == 8 and dim == LANES and nodes % 256 == 0
    assert cand_at + max(cand_at, cands) <= LANES and n * parts <= 256 and passage_tiles.shape[0] <= 256
    me = lax.axis_index("dom").astype(jnp.int32)
    stride = queries * qt + 16
    blocks = n // 4
    orders = orders_of(n)
    masks = [sources_of(o) for o in orders]

    pairs_count = queries * cands
    cap = max(2, min(pairs_count, 2 * pairs_count // n))
    slots = n * cap
    assert slots % LANES == 0 and slots <= 4 * LANES and LANES % cap == 0 and pairs_count <= 256
    half = fde // 2
    query_tokens, left_part, right_part = lax.optimization_barrier(
        (query_tokens, query_fde[:, :half], query_fde[:, half:])
    )
    packed = pl.pallas_call(
        functools.partial(prep_kernel, parts, slots, cap),
        out_shape=jax.ShapeDtypeStruct((stride, dim), jnp.bfloat16),
        in_specs=[VMEM] * 5,
        out_specs=VMEM,
        name="pack",
    )(frontier_owner, frontier_slot, cand_owner.reshape(queries, cands), cand_slot, query_tokens.reshape(queries * qt, dim))
    starts = [packed, left_part, right_part]
    stages = len(orders[0])

    @functools.cache
    def gathered(k, step):
        if step == 0:
            return starts[k]
        return jnp.concatenate([gathered(k, step - 1), arrived(k, step - 1)], axis=0)

    @functools.cache
    def arrived(k, step):
        return exchange(gathered(k, step), orders[k][step], n)

    tok = [gathered(0, stages - 1), arrived(0, stages - 1)]
    tok = [(tok[0], exchange(tok[0], 1, n)), tok[1]]

    pt = passage_tiles.shape[1]
    score = lambda *sides: pl.pallas_call(
            functools.partial(maxsim_kernel, cand_at, cands, cap),
            out_shape=jax.ShapeDtypeStruct((n // 4 * len(sides), 8, LANES), jnp.float32),
            grid_spec=pltpu.PrefetchScalarGridSpec(
                num_scalar_prefetch=2,
                grid=(),
                in_specs=[VMEM] * (len(sides) + 1),
                out_specs=VMEM,
                scratch_shapes=[
                    pltpu.VMEM((n // 4 * len(sides), LANES), jnp.int32),
                    pltpu.SMEM((n // 4 * len(sides), LANES), jnp.int32),
                    pltpu.SemaphoreType.DMA,
                ],
            ),
            compiler_params=pltpu.CompilerParams(vmem_limit_bytes=16 << 20),
            cost_estimate=pl.CostEstimate(flops=4 * len(sides) * slots * pt * qt * dim, bytes_accessed=8 << 20, transcendentals=0),
            name="maxsim",
        )(me.reshape(1), passage_len, *sides, passage_tiles)

    early = score(*tok[0])
    late, early = lax.optimization_barrier((tok[1], early))
    late_other = exchange(late, 1, n)
    maxsim = [early, score(late)]
    a_own, b_own, late_other, _ = lax.optimization_barrier((gathered(1, stages), gathered(2, stages), late_other, maxsim[1]))
    tok = [tok[0], (late, late_other)]
    maxsim.append(score(late_other))
    a_other, b_other = exchange(a_own, 1, n), exchange(b_own, 1, n)

    rows = n * 8
    full = lambda shape: pl.BlockSpec(shape, lambda i, *_: (0,) * len(shape))
    left = full((rows // 2, half))
    doc = lambda at: pl.BlockSpec((nodes, half), lambda i, *_: (0, at))
    partial = jax.ShapeDtypeStruct((rows, nodes), jnp.float32)
    cost = pl.CostEstimate(flops=2 * rows * nodes * half, bytes_accessed=2 * (rows + nodes) * half, transcendentals=0)
    first = pl.pallas_call(
        beam_kernel,
        out_shape=partial,
        grid=(1,),
        in_specs=[left, left, doc(0)],
        out_specs=full(partial.shape),
        compiler_params=pltpu.CompilerParams(vmem_limit_bytes=16 << 20),
        cost_estimate=cost,
        name="beam",
    )(a_own, a_other, doc_fde)
    codes = [*tok[0], *tok[1]]
    scored = pl.pallas_call(
        functools.partial(last_kernel, (masks, parts, cand_at, blocks)),
        out_shape=jax.ShapeDtypeStruct((n, 8, LANES), jnp.float32),
        grid_spec=pltpu.PrefetchScalarGridSpec(
            num_scalar_prefetch=1,
            grid=(1,),
            in_specs=[left, left, doc(1)] + [full(x.shape) for x in (first, *codes, *maxsim)],
            out_specs=full((n, 8, LANES)),
            scratch_shapes=[pltpu.VMEM(partial.shape, jnp.float32)],
        ),
        compiler_params=pltpu.CompilerParams(vmem_limit_bytes=24 << 20),
        cost_estimate=cost,
        name="beam_last",
    )(me.reshape(1), b_own, b_other, doc_fde, first, *codes, *maxsim)

    returned = lax.all_to_all(scored, "dom", split_axis=0, concat_axis=0, tiled=True)
    total = jnp.sum(returned, axis=0)
    beam = total[:, :cand_at].reshape(queries, rounds, front).transpose(1, 0, 2)
    return beam, total[:, cand_at : cand_at + cands]


def solution(mesh):
    in_specs = (
        P(("rep", "dom"), None),
        P("dom", None),
        P(None, ("rep", "dom"), None),
        P(None, ("rep", "dom"), None),
        P(("rep", "dom"), None, None),
        P("dom", None, None),
        P("dom"),
        P(("rep", "dom"), None, None),
        P(("rep", "dom"), None),
    )
    out_specs = (P(None, ("rep", "dom"), None), P(("rep", "dom"), None))
    return jax.shard_map(
        functools.partial(local, mesh.shape["dom"]), mesh=mesh, in_specs=in_specs, out_specs=out_specs, check_vma=False
    )
```

```python
import functools
import math

import jax
import jax.numpy as jnp
from jax import lax
from jax.experimental import pallas as pl
from jax.experimental.pallas import tpu as pltpu
from jax.sharding import PartitionSpec as P

masked_value = -1e30
LANES = 128
VMEM = pl.BlockSpec(memory_space=pltpu.VMEM)
NT = (((1,), (1,)), ((), ()))


def sources_of(order):
    masks = [0]
    for bit in order:
        masks = masks + [m ^ bit for m in masks]
    return masks


def orders_of(n):
    bits = [1 << i for i in range(1, n.bit_length() - 1)]
    far, rest = bits[-1:], bits[-3:-5:-1] + bits[:-4] + bits[-2:-1]
    assert sorted(far + rest) == bits
    return [far + rest, far + rest[-1:] + rest[:-1], far + rest[1:] + rest[:1]]


def exchange(x, bit, n):
    return lax.ppermute(x, "dom", [(i, i ^ bit) for i in range(n)])


def place(values, offset):
    w = values.shape[1]
    where = lax.broadcasted_iota(jnp.int32, (w, LANES), 0) + offset
    lane = lax.broadcasted_iota(jnp.int32, (w, LANES), 1)
    return jnp.dot(
        values.astype(jnp.float32).astype(jnp.bfloat16),
        (where == lane).astype(jnp.float32).astype(jnp.bfloat16),
        preferred_element_type=jnp.float32,
    )


def ids(shape, axis):
    return lax.broadcasted_iota(jnp.int32, shape, axis)


def exact(values):
    return values.astype(jnp.float32).astype(jnp.bfloat16)


def pick(a, b):
    return jnp.dot(exact(a), exact(b), preferred_element_type=jnp.float32)


def prep_kernel(parts, slots, cap, fo, fs, co, cs, tok, out):
    rounds, queries, front = fo.shape
    rows, cands = tok.shape[0], co.shape[1]
    pairs = queries * cands
    low_at = rounds * front
    codes = jnp.zeros((queries, LANES), jnp.float32)
    for r in range(rounds):
        codes = codes + place(fo[r] * parts + (fs[r] >> 8), r * front)
        codes = codes + place(fs[r] & 255, low_at + r * front)

    across = (ids((cands, pairs), 1) % cands == ids((cands, pairs), 0))
    mine = ids((queries, pairs), 1) // cands == ids((queries, pairs), 0)
    line = lambda v: jnp.sum(jnp.where(mine, pick(v, across), 0.0), axis=0, keepdims=True)
    owner_line, slot_line = line(co[...]), line(cs[...])
    down = ids((pairs, queries), 0) // cands == ids((pairs, queries), 1)
    here = ids((pairs, cands), 0) % cands == ids((pairs, cands), 1)
    owner = jnp.sum(jnp.where(here, pick(down, co[...]), 0.0), axis=1, keepdims=True)
    earlier = (owner == owner_line) & (ids((pairs, pairs), 1) < ids((pairs, pairs), 0))
    position = jnp.sum(jnp.where(earlier, 1.0, 0.0), axis=1, keepdims=True)
    target = (owner * cap + position).astype(jnp.int32)
    number = (ids((1, pairs), 1) + 1).astype(jnp.float32)
    table = jnp.zeros((8, LANES), jnp.float32)
    for g in range(slots // LANES):
        row = ids((8, pairs), 0)
        values = jnp.where(row == 2 * g, number, jnp.where(row == 2 * g + 1, slot_line, 0.0))
        table = table + pick(values, target == ids((pairs, LANES), 1) + g * LANES)
    out[:rows, :] = tok[...]
    out[rows:, :] = jnp.concatenate([codes, table], axis=0).astype(jnp.bfloat16)


def maxsim_kernel(cand_at, cands, cap, me_ref, lens, *refs):
    *sides, tiles, out, listed, lst, sem = refs
    blocks = out.shape[0] // len(sides)
    stride = sides[0].shape[0] // blocks
    pt = tiles.shape[1]
    qt = (stride - 16) // 8
    start = me_ref[0] * cap
    row, lane = ids((8, LANES), 0), ids((8, LANES), 1)
    group = start // LANES
    for side, ref in enumerate(sides):
        for b in range(blocks):
            table = ref[(b + 1) * stride - 16 : (b + 1) * stride, :].astype(jnp.float32)[8:]
            weight = jnp.where(row == 2 * group, 256.0, jnp.where(row == 2 * group + 1, 1.0, 0.0))
            at = side * blocks + b
            listed[at : at + 1, :] = jnp.sum(table * weight, axis=0, keepdims=True).astype(jnp.int32)
    listed[...] = pltpu.roll(listed[...], lax.rem(LANES - start % LANES, LANES), axis=1)
    copy = pltpu.make_async_copy(listed, lst, sem)
    copy.start()
    copy.wait()

    spot = jnp.where((lane >= cand_at) & (lane < cand_at + cands), row * cands + lane - cand_at, -1)
    token = ids((pt, 2 * qt), 0)
    right = ids((1, 2 * qt), 1) >= qt
    empty = jnp.zeros((qt, LANES), sides[0].dtype)

    def score(ref, b, at):
        tops, pairs = [], []
        for k in range(0, cap, 2):
            slots, tokens = [], []
            for entry in (lst[at, k], lst[at, k + 1]):
                pair = (entry >> 8) - 1
                query = jnp.maximum(pair, 0) // cands
                slots.append(entry & 255)
                tokens.append(ref[pl.ds(pl.multiple_of(b * stride + query * qt, 16), qt), :])
                pairs.append(jnp.where(pair < 0, -2, pair))
            data = jnp.concatenate([tiles[slots[0]], tiles[slots[1]]], axis=1)
            weights = jnp.concatenate(
                [jnp.concatenate([tokens[0], empty], axis=1), jnp.concatenate([empty, tokens[1]], axis=1)], axis=0
            )
            sim = lax.dot_general(data, weights, NT, preferred_element_type=jnp.float32)
            length = jnp.where(right, lens[slots[1]], lens[slots[0]])
            sim = jnp.where(token < length, sim, masked_value)
            tops.append(jnp.max(sim, axis=0, keepdims=True))
        tops = jnp.concatenate(tops, axis=0)
        first = jnp.sum(jnp.where(right, 0.0, tops), axis=1, keepdims=True) * (1.0 / qt)
        second = jnp.sum(jnp.where(right, tops, 0.0), axis=1, keepdims=True) * (1.0 / qt)
        acc = jnp.zeros((8, LANES), jnp.float32)
        for k in range(cap):
            means = second if k % 2 else first
            acc = acc + jnp.where(spot == pairs[k], means[k // 2 : k // 2 + 1, :], 0.0)
        out[at] = acc

    together = 8 // len(sides)

    def step(i, carry):
        for u in range(together):
            for side, ref in enumerate(sides):
                score(ref, together * i + u, side * blocks + together * i + u)
        return carry

    lax.fori_loop(0, blocks // together, step, 0)


def beam_kernel(own, other, doc, total):
    left = jnp.concatenate([own[...], other[...]], axis=0)
    total[...] = lax.dot_general(left, doc[...], NT, preferred_element_type=jnp.float32)


def last_kernel(cfg, me_ref, own, other, doc, first, *refs):
    masks, parts, cand_at, blocks = cfg
    codes, scores, out, last = refs[:4], refs[4:7], refs[7], refs[8]
    stride = codes[0].shape[0] // blocks
    beam_kernel(own, other, doc, last)

    me = me_ref[0]
    lane = ids((8, LANES), 1)
    nodes = last.shape[1]

    for m in masks[0]:
        for side in range(2):
            half, t = divmod(masks[0].index(m), blocks)
            table = codes[2 * half + side][(t + 1) * stride - 16 : (t + 1) * stride, :].astype(jnp.float32)[:8]
            low = pltpu.roll(table, LANES - cand_at, axis=1).astype(jnp.int32)
            table = table.astype(jnp.int32)
            owner, high = table // parts, table % parts
            slot = high * 256 + low
            within, page = slot % LANES, slot // LANES
            ats = [(side * 2 * blocks + masks[k].index(m)) * 8 for k in (1, 2)]
            rows = first[ats[0] : ats[0] + 8, :] + last[ats[1] : ats[1] + 8, :]
            found = jnp.zeros((8, LANES), jnp.float32)
            for g in range(nodes // LANES):
                here = jnp.take_along_axis(rows[:, g * LANES : (g + 1) * LANES], within, axis=1)
                found = jnp.where(page == g, here, found)
            found = jnp.where(owner == me, found, 0.0)
            out[me ^ (m + side)] = jnp.where(lane < cand_at, found, (scores[0][side * blocks + t] if half == 0 else scores[1 + side][t]))


def local(n, query_fde, doc_fde, frontier_owner, frontier_slot, query_tokens, passage_tiles, passage_len, cand_owner, cand_slot):
    rounds, queries, front = frontier_owner.shape
    cands = cand_slot.shape[1]
    nodes, fde = doc_fde.shape
    qt, dim = query_tokens.shape[1:]
    parts = nodes // 256
    cand_at = rounds * front
    assert n & (n - 1) == 0 and queries == 8 and dim == LANES and nodes % 256 == 0
    assert cand_at + max(cand_at, cands) <= LANES and n * parts <= 256 and passage_tiles.shape[0] <= 256
    me = lax.axis_index("dom").astype(jnp.int32)
    stride = queries * qt + 16
    blocks = n // 4
    orders = orders_of(n)
    masks = [sources_of(o) for o in orders]

    pairs_count = queries * cands
    cap = max(2, min(pairs_count, 2 * pairs_count // n))
    slots = n * cap
    assert slots % LANES == 0 and slots <= 4 * LANES and LANES % cap == 0 and pairs_count <= 256
    half = fde // 2
    query_tokens, left_part, right_part = lax.optimization_barrier(
        (query_tokens, query_fde[:, :half], query_fde[:, half:])
    )
    packed = pl.pallas_call(
        functools.partial(prep_kernel, parts, slots, cap),
        out_shape=jax.ShapeDtypeStruct((stride, dim), jnp.bfloat16),
        in_specs=[VMEM] * 5,
        out_specs=VMEM,
        name="pack",
    )(frontier_owner, frontier_slot, cand_owner.reshape(queries, cands), cand_slot, query_tokens.reshape(queries * qt, dim))
    starts = [packed, left_part, right_part]
    stages = len(orders[0])

    @functools.cache
    def gathered(k, step):
        if step == 0:
            return starts[k]
        return jnp.concatenate([gathered(k, step - 1), arrived(k, step - 1)], axis=0)

    @functools.cache
    def arrived(k, step):
        return exchange(gathered(k, step), orders[k][step], n)

    tok = [gathered(0, stages - 1), arrived(0, stages - 1)]
    tok = [(tok[0], exchange(tok[0], 1, n)), tok[1]]

    pt = passage_tiles.shape[1]
    score = lambda *sides: pl.pallas_call(
            functools.partial(maxsim_kernel, cand_at, cands, cap),
            out_shape=jax.ShapeDtypeStruct((n // 4 * len(sides), 8, LANES), jnp.float32),
            grid_spec=pltpu.PrefetchScalarGridSpec(
                num_scalar_prefetch=2,
                grid=(),
                in_specs=[VMEM] * (len(sides) + 1),
                out_specs=VMEM,
                scratch_shapes=[
                    pltpu.VMEM((n // 4 * len(sides), LANES), jnp.int32),
                    pltpu.SMEM((n // 4 * len(sides), LANES), jnp.int32),
                    pltpu.SemaphoreType.DMA,
                ],
            ),
            compiler_params=pltpu.CompilerParams(vmem_limit_bytes=16 << 20),
            cost_estimate=pl.CostEstimate(flops=4 * len(sides) * slots * pt * qt * dim, bytes_accessed=8 << 20, transcendentals=0),
            name="maxsim",
        )(me.reshape(1), passage_len, *sides, passage_tiles)

    early = score(*tok[0])
    late, early = lax.optimization_barrier((tok[1], early))
    late_other = exchange(late, 1, n)
    maxsim = [early, score(late)]
    a_own, b_own, late_other, _ = lax.optimization_barrier((gathered(1, stages), gathered(2, stages), late_other, maxsim[1]))
    tok = [tok[0], (late, late_other)]
    maxsim.append(score(late_other))
    a_other, b_other = exchange(a_own, 1, n), exchange(b_own, 1, n)

    rows = n * 8
    full = lambda shape: pl.BlockSpec(shape, lambda i, *_: (0,) * len(shape))
    left = full((rows // 2, half))
    doc = lambda at: pl.BlockSpec((nodes, half), lambda i, *_: (0, at))
    partial = jax.ShapeDtypeStruct((rows, nodes), jnp.float32)
    cost = pl.CostEstimate(flops=2 * rows * nodes * half, bytes_accessed=2 * (rows + nodes) * half, transcendentals=0)
    first = pl.pallas_call(
        beam_kernel,
        out_shape=partial,
        grid=(1,),
        in_specs=[left, left, doc(0)],
        out_specs=full(partial.shape),
        compiler_params=pltpu.CompilerParams(vmem_limit_bytes=16 << 20),
        cost_estimate=cost,
        name="beam",
    )(a_own, a_other, doc_fde)
    codes = [*tok[0], *tok[1]]
    scored = pl.pallas_call(
        functools.partial(last_kernel, (masks, parts, cand_at, blocks)),
        out_shape=jax.ShapeDtypeStruct((n, 8, LANES), jnp.float32),
        grid_spec=pltpu.PrefetchScalarGridSpec(
            num_scalar_prefetch=1,
            grid=(1,),
            in_specs=[left, left, doc(1)] + [full(x.shape) for x in (first, *codes, *maxsim)],
            out_specs=full((n, 8, LANES)),
            scratch_shapes=[pltpu.VMEM(partial.shape, jnp.float32)],
        ),
        compiler_params=pltpu.CompilerParams(vmem_limit_bytes=24 << 20),
        cost_estimate=cost,
        name="beam_last",
    )(me.reshape(1), b_own, b_other, doc_fde, first, *codes, *maxsim)

    returned = lax.all_to_all(scored, "dom", split_axis=0, concat_axis=0, tiled=True)
    total = jnp.sum(returned, axis=0)
    beam = total[:, :cand_at].reshape(queries, rounds, front).transpose(1, 0, 2)
    return beam, total[:, cand_at : cand_at + cands]


def solution(mesh):
    in_specs = (
        P(("rep", "dom"), None),
        P("dom", None),
        P(None, ("rep", "dom"), None),
        P(None, ("rep", "dom"), None),
        P(("rep", "dom"), None, None),
        P("dom", None, None),
        P("dom"),
        P(("rep", "dom"), None, None),
        P(("rep", "dom"), None),
    )
    out_specs = (P(None, ("rep", "dom"), None), P(("rep", "dom"), None))
    return jax.shard_map(
        functools.partial(local, mesh.shape["dom"]), mesh=mesh, in_specs=in_specs, out_specs=out_specs, check_vma=False
    )
```

```python
import functools
import math

import jax
import jax.numpy as jnp
from jax import lax
from jax.experimental import pallas as pl
from jax.experimental.pallas import tpu as pltpu
from jax.sharding import PartitionSpec as P

masked_value = -1e30
LANES = 128
VMEM = pl.BlockSpec(memory_space=pltpu.VMEM)
NT = (((1,), (1,)), ((), ()))


def sources_of(order):
    masks = [0]
    for bit in order:
        masks = masks + [m ^ bit for m in masks]
    return masks


def orders_of(n):
    bits = [1 << i for i in range(1, n.bit_length() - 1)]
    far, rest = bits[-1:], bits[-3:-5:-1] + bits[:-4] + bits[-2:-1]
    assert sorted(far + rest) == bits
    return [far + rest, far + rest[-1:] + rest[:-1], far + rest[1:] + rest[:1]]


def exchange(x, bit, n):
    return lax.ppermute(x, "dom", [(i, i ^ bit) for i in range(n)])


def place(values, offset):
    w = values.shape[1]
    where = lax.broadcasted_iota(jnp.int32, (w, LANES), 0) + offset
    lane = lax.broadcasted_iota(jnp.int32, (w, LANES), 1)
    return jnp.dot(
        values.astype(jnp.float32).astype(jnp.bfloat16),
        (where == lane).astype(jnp.float32).astype(jnp.bfloat16),
        preferred_element_type=jnp.float32,
    )


def ids(shape, axis):
    return lax.broadcasted_iota(jnp.int32, shape, axis)


def exact(values):
    return values.astype(jnp.float32).astype(jnp.bfloat16)


def pick(a, b):
    return jnp.dot(exact(a), exact(b), preferred_element_type=jnp.float32)


def prep_kernel(parts, slots, cap, fo, fs, co, cs, tok, out):
    rounds, queries, front = fo.shape
    rows, cands = tok.shape[0], co.shape[1]
    pairs = queries * cands
    low_at = rounds * front
    codes = jnp.zeros((queries, LANES), jnp.float32)
    for r in range(rounds):
        codes = codes + place(fo[r] * parts + (fs[r] >> 8), r * front)
        codes = codes + place(fs[r] & 255, low_at + r * front)

    across = (ids((cands, pairs), 1) % cands == ids((cands, pairs), 0))
    mine = ids((queries, pairs), 1) // cands == ids((queries, pairs), 0)
    line = lambda v: jnp.sum(jnp.where(mine, pick(v, across), 0.0), axis=0, keepdims=True)
    owner_line, slot_line = line(co[...]), line(cs[...])
    down = ids((pairs, queries), 0) // cands == ids((pairs, queries), 1)
    here = ids((pairs, cands), 0) % cands == ids((pairs, cands), 1)
    owner = jnp.sum(jnp.where(here, pick(down, co[...]), 0.0), axis=1, keepdims=True)
    earlier = (owner == owner_line) & (ids((pairs, pairs), 1) < ids((pairs, pairs), 0))
    position = jnp.sum(jnp.where(earlier, 1.0, 0.0), axis=1, keepdims=True)
    target = (owner * cap + position).astype(jnp.int32)
    number = (ids((1, pairs), 1) + 1).astype(jnp.float32)
    table = jnp.zeros((8, LANES), jnp.float32)
    for g in range(slots // LANES):
        row = ids((8, pairs), 0)
        values = jnp.where(row == 2 * g, number, jnp.where(row == 2 * g + 1, slot_line, 0.0))
        table = table + pick(values, target == ids((pairs, LANES), 1) + g * LANES)
    out[:rows, :] = tok[...]
    out[rows:, :] = jnp.concatenate([codes, table], axis=0).astype(jnp.bfloat16)


def maxsim_kernel(cand_at, cands, cap, lens, *refs):
    *sides, tiles, out, listed, lst, sem = refs
    blocks = out.shape[0] // len(sides)
    stride = sides[0].shape[0] // blocks
    pt = tiles.shape[1]
    qt = (stride - 16) // 8
    start = lens[tiles.shape[0]] * cap
    row, lane = ids((8, LANES), 0), ids((8, LANES), 1)
    group = start // LANES
    for side, ref in enumerate(sides):
        for b in range(blocks):
            table = ref[(b + 1) * stride - 16 : (b + 1) * stride, :].astype(jnp.float32)[8:]
            weight = jnp.where(row == 2 * group, 256.0, jnp.where(row == 2 * group + 1, 1.0, 0.0))
            at = side * blocks + b
            listed[at : at + 1, :] = jnp.sum(table * weight, axis=0, keepdims=True).astype(jnp.int32)
    listed[...] = pltpu.roll(listed[...], lax.rem(LANES - start % LANES, LANES), axis=1)
    copy = pltpu.make_async_copy(listed, lst, sem)
    copy.start()
    copy.wait()

    spot = jnp.where((lane >= cand_at) & (lane < cand_at + cands), row * cands + lane - cand_at, -1)
    token = ids((pt, 2 * qt), 0)
    right = ids((1, 2 * qt), 1) >= qt
    empty = jnp.zeros((qt, LANES), sides[0].dtype)

    def score(ref, b, at):
        tops, pairs = [], []
        for k in range(0, cap, 2):
            slots, tokens = [], []
            for entry in (lst[at, k], lst[at, k + 1]):
                pair = (entry >> 8) - 1
                query = jnp.maximum(pair, 0) // cands
                slots.append(entry & 255)
                tokens.append(ref[pl.ds(pl.multiple_of(b * stride + query * qt, 16), qt), :])
                pairs.append(jnp.where(pair < 0, -2, pair))
            data = jnp.concatenate([tiles[slots[0]], tiles[slots[1]]], axis=1)
            weights = jnp.concatenate(
                [jnp.concatenate([tokens[0], empty], axis=1), jnp.concatenate([empty, tokens[1]], axis=1)], axis=0
            )
            sim = lax.dot_general(data, weights, NT, preferred_element_type=jnp.float32)
            length = jnp.where(right, lens[slots[1]], lens[slots[0]])
            sim = jnp.where(token < length, sim, masked_value)
            tops.append(jnp.max(sim, axis=0, keepdims=True))
        tops = jnp.concatenate(tops, axis=0)
        first = jnp.sum(jnp.where(right, 0.0, tops), axis=1, keepdims=True) * (1.0 / qt)
        second = jnp.sum(jnp.where(right, tops, 0.0), axis=1, keepdims=True) * (1.0 / qt)
        acc = jnp.zeros((8, LANES), jnp.float32)
        for k in range(cap):
            means = second if k % 2 else first
            acc = acc + jnp.where(spot == pairs[k], means[k // 2 : k // 2 + 1, :], 0.0)
        out[at] = acc

    together = 8 // len(sides)

    def step(i, carry):
        for u in range(together):
            for side, ref in enumerate(sides):
                score(ref, together * i + u, side * blocks + together * i + u)
        return carry

    lax.fori_loop(0, blocks // together, step, 0)


def beam_kernel(own, other, doc, total):
    left = jnp.concatenate([own[...], other[...]], axis=0)
    total[...] = lax.dot_general(left, doc[...], NT, preferred_element_type=jnp.float32)


def last_kernel(cfg, me_ref, own, other, doc, first, *refs):
    masks, parts, cand_at, blocks = cfg
    codes, scores, out, last = refs[:4], refs[4:7], refs[7], refs[8]
    stride = codes[0].shape[0] // blocks
    beam_kernel(own, other, doc, last)

    me = me_ref[0]
    lane = ids((8, LANES), 1)
    nodes = last.shape[1]

    for m in masks[0]:
        for side in range(2):
            half, t = divmod(masks[0].index(m), blocks)
            table = codes[2 * half + side][(t + 1) * stride - 16 : (t + 1) * stride, :].astype(jnp.float32)[:8]
            low = pltpu.roll(table, LANES - cand_at, axis=1).astype(jnp.int32)
            table = table.astype(jnp.int32)
            owner, high = table // parts, table % parts
            slot = high * 256 + low
            within, page = slot % LANES, slot // LANES
            ats = [(side * 2 * blocks + masks[k].index(m)) * 8 for k in (1, 2)]
            rows = first[ats[0] : ats[0] + 8, :] + last[ats[1] : ats[1] + 8, :]
            found = jnp.zeros((8, LANES), jnp.float32)
            for g in range(nodes // LANES):
                here = jnp.take_along_axis(rows[:, g * LANES : (g + 1) * LANES], within, axis=1)
                found = jnp.where(page == g, here, found)
            found = jnp.where(owner == me, found, 0.0)
            out[me ^ (m + side)] = jnp.where(lane < cand_at, found, (scores[0][side * blocks + t] if half == 0 else scores[1 + side][t]))


def local(n, query_fde, doc_fde, frontier_owner, frontier_slot, query_tokens, passage_tiles, passage_len, cand_owner, cand_slot):
    rounds, queries, front = frontier_owner.shape
    cands = cand_slot.shape[1]
    nodes, fde = doc_fde.shape
    qt, dim = query_tokens.shape[1:]
    parts = nodes // 256
    cand_at = rounds * front
    assert n & (n - 1) == 0 and queries == 8 and dim == LANES and nodes % 256 == 0
    assert cand_at + max(cand_at, cands) <= LANES and n * parts <= 256 and passage_tiles.shape[0] <= 256
    me = lax.axis_index("dom").astype(jnp.int32)
    stride = queries * qt + 16
    blocks = n // 4
    orders = orders_of(n)
    masks = [sources_of(o) for o in orders]

    pairs_count = queries * cands
    cap = max(2, min(pairs_count, 2 * pairs_count // n))
    slots = n * cap
    assert slots % LANES == 0 and slots <= 4 * LANES and LANES % cap == 0 and pairs_count <= 256
    half = fde // 2
    query_tokens, left_part, right_part = lax.optimization_barrier(
        (query_tokens, query_fde[:, :half], query_fde[:, half:])
    )
    packed = pl.pallas_call(
        functools.partial(prep_kernel, parts, slots, cap),
        out_shape=jax.ShapeDtypeStruct((stride, dim), jnp.bfloat16),
        in_specs=[VMEM] * 5,
        out_specs=VMEM,
        name="pack",
    )(frontier_owner, frontier_slot, cand_owner.reshape(queries, cands), cand_slot, query_tokens.reshape(queries * qt, dim))
    starts = [packed, left_part, right_part]
    stages = len(orders[0])

    @functools.cache
    def gathered(k, step):
        if step == 0:
            return starts[k]
        return jnp.concatenate([gathered(k, step - 1), arrived(k, step - 1)], axis=0)

    @functools.cache
    def arrived(k, step):
        return exchange(gathered(k, step), orders[k][step], n)

    tok = [gathered(0, stages - 1), arrived(0, stages - 1)]
    tok = [(tok[0], exchange(tok[0], 1, n)), tok[1]]

    pt = passage_tiles.shape[1]
    scalars = jnp.concatenate([passage_len, me.reshape(1)])
    score = lambda *sides: pl.pallas_call(
            functools.partial(maxsim_kernel, cand_at, cands, cap),
            out_shape=jax.ShapeDtypeStruct((n // 4 * len(sides), 8, LANES), jnp.float32),
            grid_spec=pltpu.PrefetchScalarGridSpec(
                num_scalar_prefetch=1,
                grid=(),
                in_specs=[VMEM] * (len(sides) + 1),
                out_specs=VMEM,
                scratch_shapes=[
                    pltpu.VMEM((n // 4 * len(sides), LANES), jnp.int32),
                    pltpu.SMEM((n // 4 * len(sides), LANES), jnp.int32),
                    pltpu.SemaphoreType.DMA,
                ],
            ),
            compiler_params=pltpu.CompilerParams(vmem_limit_bytes=16 << 20),
            cost_estimate=pl.CostEstimate(flops=4 * len(sides) * slots * pt * qt * dim, bytes_accessed=8 << 20, transcendentals=0),
            name="maxsim",
        )(scalars, *sides, passage_tiles)

    early = score(*tok[0])
    late, early = lax.optimization_barrier((tok[1], early))
    late_other = exchange(late, 1, n)
    maxsim = [early, score(late)]
    a_own, b_own, late_other, _ = lax.optimization_barrier((gathered(1, stages), gathered(2, stages), late_other, maxsim[1]))
    tok = [tok[0], (late, late_other)]
    maxsim.append(score(late_other))
    a_other, b_other = exchange(a_own, 1, n), exchange(b_own, 1, n)

    rows = n * 8
    full = lambda shape: pl.BlockSpec(shape, lambda i, *_: (0,) * len(shape))
    left = full((rows // 2, half))
    doc = lambda at: pl.BlockSpec((nodes, half), lambda i, *_: (0, at))
    partial = jax.ShapeDtypeStruct((rows, nodes), jnp.float32)
    cost = pl.CostEstimate(flops=2 * rows * nodes * half, bytes_accessed=2 * (rows + nodes) * half, transcendentals=0)
    first = pl.pallas_call(
        beam_kernel,
        out_shape=partial,
        grid=(1,),
        in_specs=[left, left, doc(0)],
        out_specs=full(partial.shape),
        compiler_params=pltpu.CompilerParams(vmem_limit_bytes=16 << 20),
        cost_estimate=cost,
        name="beam",
    )(a_own, a_other, doc_fde)
    codes = [*tok[0], *tok[1]]
    scored = pl.pallas_call(
        functools.partial(last_kernel, (masks, parts, cand_at, blocks)),
        out_shape=jax.ShapeDtypeStruct((n, 8, LANES), jnp.float32),
        grid_spec=pltpu.PrefetchScalarGridSpec(
            num_scalar_prefetch=1,
            grid=(1,),
            in_specs=[left, left, doc(1)] + [full(x.shape) for x in (first, *codes, *maxsim)],
            out_specs=full((n, 8, LANES)),
            scratch_shapes=[pltpu.VMEM(partial.shape, jnp.float32)],
        ),
        compiler_params=pltpu.CompilerParams(vmem_limit_bytes=24 << 20),
        cost_estimate=cost,
        name="beam_last",
    )(me.reshape(1), b_own, b_other, doc_fde, first, *codes, *maxsim)

    returned = lax.all_to_all(scored, "dom", split_axis=0, concat_axis=0, tiled=True)
    total = jnp.sum(returned, axis=0)
    beam = jnp.stack([total[:, r * front : (r + 1) * front] for r in range(rounds)])
    return beam, total[:, cand_at : cand_at + cands]


def solution(mesh):
    in_specs = (
        P(("rep", "dom"), None),
        P("dom", None),
        P(None, ("rep", "dom"), None),
        P(None, ("rep", "dom"), None),
        P(("rep", "dom"), None, None),
        P("dom", None, None),
        P("dom"),
        P(("rep", "dom"), None, None),
        P(("rep", "dom"), None),
    )
    out_specs = (P(None, ("rep", "dom"), None), P(("rep", "dom"), None))
    return jax.shard_map(
        functools.partial(local, mesh.shape["dom"]), mesh=mesh, in_specs=in_specs, out_specs=out_specs, check_vma=False
    )
```
